32 devices in a mesh: mem: 8 (over z, y), band: 4 (over x, core).
Axes of the slice: x: 2, y: 2, z: 4, core: 2. Of those that a mesh axis runs over, the one named last changes fastest.
Arguments:
- alpha: bfloat16 [16, 4, 320, 720], P('mem', None, 'band'), may hold values from -6 to 6
- static_ctl: bfloat16 [4, 320, 720], P(None, 'band'), may hold values from -6 to 6
- perturbations: bfloat16 [16, 4, 320, 720], P('mem', None, None, 'band'), may hold values from -6 to 6
- static_std: float32 [4, 320, 720], P(None, None, 'band'), may hold values from 0.5 to 2
- lon_root: bfloat16 [720, 720], replicated, may hold values from -0.11 to 1.11
- lat_root: bfloat16 [320, 320], replicated, may hold values from -0.11 to 1.11
- jacobian: bfloat16 [32, 4, 320, 720], P(None, None, 'mem', 'band'), may hold values from -3 to 3
- obs_count: int32 [320, 720], P('mem', 'band'), may hold values from 1 to 6
- channel_mask: int32 [32, 320, 720], P(None, 'mem', 'band'), may hold values 0 or 1
- channel_error: float32 [32], replicated, may hold values from 1 to 2
- member_weight: int32 [16], replicated, may hold values from 1 to 4
Outputs:
- grad_alpha: float32 [16, 4, 320, 720], P('mem', None, 'band')
- grad_static: float32 [4, 320, 720], P(None, 'band')
The draws below stay inside these ranges and needn't reach their ends.
All inputs are finite; a program needn't handle non-finite values. No bound on the sum of `channel_mask` on one device may be relied on, other than what follows from the above.
Results may differ from the reference program's by a relative error of at most 0.0055.
Values may be sent and summed in bfloat16 or wider, within the bound.
No kernel may reach another device: no remote copies, remote signals or barrier semaphores. Data moves between devices by JAX's collectives and lax.ppermute only.
A program may use at most 64 MiB of HBM per device.

```python
import math
import jax
import jax.numpy as jnp
from jax import lax

S = 4
CH = 32
LAT = 320
LON = 720
MEM = 16


def root_matrix(key, count, periodic):
    index = jnp.arange(count)
    gap = jnp.abs(index[:, None] - index[None, :])
    if periodic:
        gap = jnp.minimum(gap, count - gap)
    reach = count / 2.0
    shape = jnp.exp(-(gap.astype(jnp.float32) / reach) ** 2)
    rough = jax.random.uniform(key, (count, count), jnp.float32, -1.0, 1.0)
    matrix = jnp.eye(count, dtype=jnp.float32) + 0.8 / math.sqrt(count) * shape * rough
    return matrix.astype(jnp.bfloat16)


def draw_lon_root(key, part):
    return root_matrix(jax.random.fold_in(key, 11), LON, True)


def draw_lat_root(key, part):
    return root_matrix(jax.random.fold_in(key, 23), LAT, False)


def touch_ends(array, key, smallest, high):
    spot = [jax.random.randint(jax.random.fold_in(key, axis), (), 0, length) for axis, length in enumerate(array.shape)]
    widest = array.shape.index(max(array.shape))
    next_to = spot[:widest] + [(spot[widest] + 1) % array.shape[widest]] + spot[widest + 1:]
    return array.at[tuple(spot)].set(smallest).at[tuple(next_to)].set(high)


def raised(array, stream_key, source, target, blocks, factor):
    owner, partner = [(jnp.arange(array.shape[axis_at]) // (array.shape[axis_at] // blocks)).reshape([-1 if axis == axis_at else 1 for axis in range(array.ndim)]) for axis_at in (source, target)]
    chosen = jax.random.permutation(stream_key, blocks)[partner]
    strong = (owner == chosen) | (owner == (partner + blocks // 2) % blocks)
    return jnp.where(strong, factor * array, array)


def block_scale(rng, shape, shards, smallest, high):
    gain, own = 1.0, jax.random.fold_in(rng, 6)
    for position, shards_of in shards:
        steps = jnp.exp(jax.random.uniform(jax.random.fold_in(own, position), (shards_of,), jnp.float32, smallest / len(shards), high / len(shards)))
        gain = gain * jnp.repeat(steps, shape[position] // shards_of).reshape([-1 if axis == position else 1 for axis in range(len(shape))])
    return gain


def gaussian(rng, shape, scale, most, split=(), kind=jnp.bfloat16):
    values = scale * jax.random.normal(rng, shape, jnp.float32)
    if split:
        values = values * block_scale(rng, shape, split, -0.22, 0.18)
    return jnp.clip(values, -most, most).astype(kind)


def heavy_noise(own_key, extent, scale, bound, shards, heavy, held_as=jnp.bfloat16):
    result = scale * jax.random.normal(own_key, extent, jnp.float32)
    if shards:
        result = result * block_scale(own_key, extent, shards, -0.22, 0.18)
    return jnp.clip(raised(result, jax.random.fold_in(own_key, 3), *heavy), -bound, bound).astype(held_as)


def setup_inputs(seed: int = 0) -> dict:
    key_of = jax.random.split(jax.random.key(seed), 12)
    alpha = gaussian(key_of[0], (MEM, S, LAT, LON), 1.0, 6.0, ((0, 8), (2, 4)))
    static_ctl = gaussian(key_of[1], (S, LAT, LON), 1.0, 6.0, ((1, 4),))
    perturbations = heavy_noise(key_of[2], (MEM, S, LAT, LON), 1.0, 6.0, ((0, 8), (3, 4)), (0, 2, 8, 2.0))
    static_std = jnp.clip(jnp.exp(math.log(2.0) - 1.3862944 * jax.random.uniform(key_of[3], (S, LAT, LON), jnp.float32) ** block_scale(key_of[3], (S, LAT, LON), ((2, 4),), -0.2, 0.2)), 0.5, 2.0)
    lon_root = draw_lon_root(jax.random.fold_in(key_of[11], 71), 0)
    lat_root = draw_lat_root(jax.random.fold_in(key_of[11], 71), 0)
    jacobian = gaussian(key_of[6], (CH, S, LAT, LON), S ** -0.5, 3.0, ((2, 8), (3, 4)))
    obs_count = touch_ends(jax.random.randint(key_of[7], (LAT, LON), 1, 7), jax.random.fold_in(key_of[7], 1), 1, 6).astype(jnp.int32)
    channel_mask = touch_ends((jax.random.randint(key_of[8], (CH, LAT, LON), 0, 4) < 3).astype(jnp.int32), jax.random.fold_in(key_of[8], 1), 0, 1)
    channel_error = jnp.clip(jnp.exp(jax.random.uniform(key_of[9], (CH,), jnp.float32, math.log(1.0), math.log(2.0))), 1.0, 2.0)
    member_weight = touch_ends(jax.random.randint(key_of[10], (MEM,), 1, 5), jax.random.fold_in(key_of[10], 1), 1, 4).astype(jnp.int32)
    return {"alpha": alpha, "static_ctl": static_ctl, "perturbations": perturbations, "static_std": static_std, "lon_root": lon_root, "lat_root": lat_root, "jacobian": jacobian, "obs_count": obs_count, "channel_mask": channel_mask, "channel_error": channel_error, "member_weight": member_weight}


def correlate(field, lon_root, lat_root):
    along_lon = jnp.dot(field, lon_root, preferred_element_type=jnp.float32).astype(jnp.bfloat16)
    return jnp.einsum('ij,sjk->sik', lat_root.astype(jnp.float32), along_lon.astype(jnp.float32))

def correlate_adjoint(field, lon_root, lat_root):
    back_lat = jnp.einsum('ji,sjk->sik', lat_root.astype(jnp.float32), field.astype(jnp.float32)).astype(jnp.bfloat16)
    return jnp.einsum('sil,jl->sij', back_lat.astype(jnp.float32), lon_root.astype(jnp.float32))

def reference(alpha, static_ctl, perturbations, static_std, lon_root, lat_root, jacobian, obs_count, channel_mask, channel_error, member_weight):
    weights = member_weight.astype(jnp.float32)
    coef = weights / jnp.sqrt(jnp.sum(weights * weights))

    def add_member(total, item):
        field, spread, factor = item
        term = 0.8 * factor * spread.astype(jnp.float32) * correlate(field, lon_root, lat_root)
        return (total + term, None)
    start = jnp.zeros((S, LAT, LON), jnp.float32)
    ensemble_sum, _ = lax.scan(add_member, start, (alpha, perturbations, coef))
    increment = ensemble_sum + 0.6 * static_std * correlate(static_ctl, lon_root, lat_root)
    obs_weight = channel_mask.astype(jnp.float32) * obs_count.astype(jnp.float32)[None] / (channel_error * channel_error)[:, None, None]
    jac_full = jacobian.astype(jnp.float32)
    radiance = lax.optimization_barrier(jnp.sum(jac_full * increment[None], axis=1))
    obs_gradient = lax.optimization_barrier(jnp.sum(jac_full * (obs_weight * radiance)[:, None], axis=0)).astype(jnp.bfloat16)
    gradient_full = obs_gradient.astype(jnp.float32)

    def member_grad(item):
        field, spread, factor = item
        adjoint_field = (0.8 * factor * spread.astype(jnp.float32) * gradient_full).astype(jnp.bfloat16)
        return field.astype(jnp.float32) + correlate_adjoint(adjoint_field, lon_root, lat_root)
    grad_alpha = lax.map(member_grad, (alpha, perturbations, coef))
    static_adjoint = (0.6 * static_std * gradient_full).astype(jnp.bfloat16)
    grad_static = static_ctl.astype(jnp.float32) + correlate_adjoint(static_adjoint, lon_root, lat_root)
    return (grad_alpha, grad_static)
```

```python
import functools
import math

import jax
import jax.numpy as jnp
from jax import lax
from jax.experimental import pallas as pl
from jax.experimental.pallas import tpu as pltpu
from jax.sharding import PartitionSpec as P

F32 = jnp.float32
BF16 = jnp.bfloat16
VMEM = pl.BlockSpec(memory_space=pltpu.VMEM)
SMEM = pl.BlockSpec(memory_space=pltpu.SMEM)
NT = (((1,), (1,)), ((), ()))


def up(n, m):
    return -(-n // m) * m


def call(kernel, out_shapes, n_smem, *args, scratch=(), flops=0, vmem=24 << 20):
    specs = [SMEM] * n_smem + [VMEM] * (len(args) - n_smem)
    size = sum(math.prod(a.shape) * a.dtype.itemsize for a in args)
    size += sum(math.prod(o.shape) * o.dtype.itemsize for o in out_shapes)
    return pl.pallas_call(
        kernel,
        out_shape=out_shapes,
        in_specs=specs,
        out_specs=[VMEM] * len(out_shapes),
        scratch_shapes=list(scratch),
        compiler_params=pltpu.CompilerParams(vmem_limit_bytes=vmem),
        cost_estimate=pl.CostEstimate(flops=flops, bytes_accessed=size, transcendentals=0),
    )(*args)


def struct(shape, dtype):
    return jax.ShapeDtypeStruct(tuple(shape), dtype)


def dot(a, b):
    return jnp.dot(a, b, preferred_element_type=F32)


def dot_nt(a, b):
    return lax.dot_general(a, b, NT, preferred_element_type=F32)


def iota(shape, axis):
    return lax.broadcasted_iota(jnp.int32, shape, axis)


class Chunk:
    def __init__(self, start, width, slot):
        self.start, self.width, self.slot = start, width, slot

    def pack(self, pieces):
        if self.slot == self.width:
            return jnp.concatenate([p[:, self.start : self.start + self.width] for p in pieces], 1)
        out = []
        for p in pieces:
            out.append(p[:, self.start : self.start + self.width])
            out.append(jnp.zeros((p.shape[0], self.slot - self.width), p.dtype))
        return jnp.concatenate(out, 1)

    def take(self, x, i):
        return x[:, i * self.slot : (i + 1) * self.slot]


def lon_kernel(ck, bands, share, alpha, static, root, *outs):
    w_ref, x_refs = outs[0], outs[1:]
    members, species, rows, lon = alpha.shape
    mine = lon // bands
    rank, me = lax.axis_index("mem"), lax.axis_index("band")
    lane = iota((lon, bands * ck.slot), 1)
    source = ((lane // ck.slot) ^ me) * mine + ck.start + lane % ck.slot
    pick = (iota((lon, bands * ck.slot), 0) == source) & (lane % ck.slot < ck.width)
    w = dot(root[...], pick.astype(F32).astype(BF16)).astype(BF16)
    w_ref[...] = w
    count, copies, padded = share
    first = (rank // copies) * count
    t = iota((padded, rows), 0)
    select = (iota((padded, rows), 1) == first + t) & (t < count) & (rank % copies == 0)
    select = select.astype(F32).astype(BF16)
    extra = [dot(select, static[s]).astype(BF16) for s in range(species)]
    field = jnp.concatenate([alpha[...].reshape(members * species * rows, lon)] + extra, 0)
    y = dot(field, w)
    for k in range(bands):
        for m in range(members):
            parts = [ck.take(y[(m * species + s) * rows : (m * species + s + 1) * rows], k) for s in range(species)]
            x_refs[k][m * rows : (m + 1) * rows, :] = jnp.concatenate(parts, 1).astype(BF16)
        top = members * species * rows
        parts = [ck.take(y[top + s * padded : top + (s + 1) * padded], k) for s in range(species)]
        x_refs[k][members * rows : members * rows + padded, :] = jnp.concatenate(parts, 1).astype(BF16)


def prep_kernel(ck, bands, share, pert, std, lat, pert_b, std_b, lat_k, lat_t, lat_s):
    members, species, height, _ = pert.shape
    total = lat.shape[1]
    rows = total // bands
    rank, me = lax.axis_index("mem"), lax.axis_index("band")
    for m in range(members):
        pert_b[m] = ck.pack([pert[m, s].astype(F32) for s in range(species)]).astype(BF16)
    std_b[...] = 0.6 * ck.pack([std[s] for s in range(species)])
    row = iota((total, total), 0)
    order = (iota((total, total), 1) == ((row // rows) ^ me) * rows + row % rows).astype(F32).astype(BF16)
    lat_k[...] = dot_nt(lat[...], order).astype(BF16)
    lat_t[...] = dot_nt(order, lat[...]).astype(BF16)
    count, copies, padded = share
    row = iota((bands * padded, total), 0)
    t = row % padded
    source = ((row // padded) ^ me) * rows + (rank // copies) * count + t
    pick = (iota((bands * padded, total), 1) == source) & (t < count) & (rank % copies == 0)
    lat_s[...] = dot_nt(lat[...], pick.astype(F32).astype(BF16)).astype(BF16)


def normal_kernel(chunks, error, jac, count, mask, *outs):
    channels, species, rows, lon = jac.shape
    pairs = [(s, t) for s in range(species) for t in range(s, species)]
    seen = count[...].astype(F32)

    def step(c, totals):
        weight = mask[c].astype(F32) * seen * (1.0 / (error[c] * error[c]))
        j = [jac[c, s].astype(F32) for s in range(species)]
        scaled = [weight * x for x in j]
        return tuple(total + scaled[s] * j[t] for total, (s, t) in zip(totals, pairs))

    zero = tuple(jnp.zeros((rows, lon), F32) for _ in pairs)
    sums = dict(zip(pairs, lax.fori_loop(0, channels, step, zero)))
    for ck, out in zip(chunks, outs):
        for d in range(species):
            parts = [sums[tuple(sorted((s, (s + d) % species)))] for s in range(species)]
            packed = ck.pack(parts)
            extra = out.shape[1] - rows
            if extra:
                packed = jnp.concatenate([packed, jnp.zeros((extra, packed.shape[1]), F32)], 0)
            out[d] = packed


def lat_kernel(ck, bands, height, coef, lat_k, lat_s, pert, std, *refs):
    x_refs, (own, sent), (total,) = refs[:bands], refs[bands : bands + 2], refs[bands + 2 :]
    members = pert.shape[0]
    rows = lat_k.shape[1] // bands
    rank = lax.axis_index("mem")
    z = jnp.concatenate([x[members * rows :, :] for x in x_refs], 0)
    if len(std.shape) == 3:
        scale = 0.6 * ck.pack([std[s] for s in range(std.shape[0])])
    else:
        scale = std[...]
    acc = scale * dot(lat_s[...], z)
    for m in range(members):
        if len(pert.shape) == 4:
            p = ck.pack([pert[m, s].astype(F32) for s in range(pert.shape[1])])
        else:
            p = pert[m].astype(F32)
        z = jnp.concatenate([x[m * rows : (m + 1) * rows, :] for x in x_refs], 0)
        acc += coef[m] * p * dot(lat_k[...], z)
    total[...] = acc
    half = own.shape[0]
    for j in range(half):
        for ref, k in ((own, 2 * j), (sent, 2 * j + 1)):
            at = pl.multiple_of((rank ^ k) * height, 8)
            ref[j] = total[pl.ds(at, height), :].astype(ref.dtype)


def pair_kernel(own, got, first, *others):
    first[...] = own[0] + got[0].astype(F32)
    for j, out in enumerate(others):
        out[...] = (own[j + 1] + got[j + 1].astype(F32)).astype(BF16)


def pixel_kernel(ck, species, normal, first, *refs):
    got, out = refs[:-1], refs[-1]
    inc = first[...]
    for ref in got:
        inc = inc + ref[...].astype(F32)
    g = normal[0] * inc
    for d in range(1, species):
        at = d * ck.slot
        g += normal[d] * jnp.concatenate([inc[:, at:], inc[:, :at]], 1)
    out[...] = g.astype(BF16)


def back_kernel(ck, bands, half, coef, lat_t, pert, std, near, far, *refs):
    outs, full = refs[:bands], refs[bands]
    members = pert.shape[0]
    height = near.shape[1]
    rows = lat_t.shape[0] // bands
    rank = lax.axis_index("mem")
    for j in range(half):
        for ref, k in ((near, 2 * j), (far, 2 * j + 1)):
            at = pl.multiple_of((rank ^ k) * height, 8)
            full[pl.ds(at, height), :] = ref[j].astype(F32)
    g = full[...]
    for m in range(members + 1):
        if m < members:
            if len(pert.shape) == 4:
                p = ck.pack([pert[m, s].astype(F32) for s in range(pert.shape[1])])
            else:
                p = pert[m].astype(F32)
            adjoint = coef[m] * p * g
        elif len(std.shape) == 3:
            adjoint = 0.6 * ck.pack([std[s] for s in range(std.shape[0])]) * g
        else:
            adjoint = std[...] * g
        y = dot(lat_t[...], adjoint.astype(BF16)).astype(BF16)
        for k in range(bands):
            outs[k][m * rows : (m + 1) * rows, :] = y[k * rows : (k + 1) * rows]


def out_kernel(chunks, bands, species, alpha, static, *refs):
    n = len(chunks)
    ws, xs, (grad_alpha, grad_static) = refs[:n], refs[n : n + n * bands], refs[-2:]
    members, _, rows, _ = alpha.shape
    s = pl.program_id(0)
    w = jnp.concatenate([ref[...] for ref in ws], 1)
    for fixed in range(species):
        @pl.when(s == fixed)
        def _():
            tiles = []
            for i, ck in enumerate(chunks):
                pieces = [ck.take(xs[i * bands + k][...].astype(F32), fixed) for k in range(bands)]
                tiles.append(jnp.concatenate(pieces, 1))
            left = jnp.concatenate(tiles, 1).astype(BF16)
            y = dot_nt(left, w)
            for m in range(members):
                grad_alpha[m, 0] = alpha[m, 0].astype(F32) + y[m * rows : (m + 1) * rows]
            grad_static[0] = static[0].astype(F32) + y[members * rows :]


def shards(bands, ranks, *args):
    alpha, static_ctl, perturbations, static_std, lon_root, lat_root = args[:6]
    jacobian, obs_count, channel_mask, channel_error, member_weight = args[6:]
    members, species, rows, lon = alpha.shape
    total = lat_root.shape[0]
    mine = lon // bands
    pixel_rows = total // ranks
    height = up(pixel_rows, 8)
    padded_total = ranks * height
    groups = math.gcd(ranks, rows)
    share = (rows // groups, ranks // groups, up(rows // groups, 16))
    half = ranks // 2
    chunks = [Chunk(0, 128, 128), Chunk(128, mine - 128, 64)]

    def send(x, axis, k):
        n = bands if axis == "band" else ranks
        return lax.ppermute(x, axis, [(i, i ^ k) for i in range(n)])

    def pad_lat(x, axis):
        if height == pixel_rows:
            return x
        shape = list(x.shape)
        x = x.reshape(shape[:axis] + [ranks, pixel_rows] + shape[axis + 1 :])
        widths = [(0, 0)] * x.ndim
        widths[axis + 1] = (0, height - pixel_rows)
        shape[axis] = padded_total
        return jnp.pad(x, widths).reshape(shape)

    weights = member_weight.astype(F32)
    coef = weights / jnp.sqrt(jnp.sum(weights * weights))
    scaled = 0.8 * lax.dynamic_slice_in_dim(coef, lax.axis_index("mem") * members, members, 0)

    sent_rows = members * rows + share[2]
    roots, fields = [], []
    for ck in chunks:
        lanes = species * ck.slot
        outs = [struct((lon, bands * ck.slot), BF16)] + [struct((sent_rows, lanes), BF16)] * bands

        got = call(
            functools.partial(lon_kernel, ck, bands, share), outs, 0,
            alpha, static_ctl, lon_root, flops=2 * 704 * lon * lanes,
        )
        roots.append(got[0])
        fields.append([got[1]] + [send(got[1 + k], "band", k) for k in range(1, bands)])

    pert = pad_lat(perturbations, 2)
    std = pad_lat(static_std, 1)
    lat = pad_lat(lat_root, 0)
    last = chunks[1]
    lanes = species * last.slot
    outs = [
        struct((members, padded_total, lanes), BF16),
        struct((padded_total, lanes), F32),
        struct((padded_total, total), BF16),
        struct((total, padded_total), BF16),
        struct((padded_total, bands * share[2]), BF16),
    ]
    pert_b, std_b, lat_k, lat_t, lat_s = call(
        functools.partial(prep_kernel, last, bands, share), outs, 0, pert, std, lat, flops=10**8
    )
    outs = [struct((species, height, species * ck.slot), F32) for ck in chunks]
    normals = call(
        functools.partial(normal_kernel, chunks), outs, 1,
        channel_error, jacobian, obs_count, channel_mask, flops=10**8,
    )
    perts, stds = [pert, pert_b], [std, std_b]

    sums = []
    for i, ck in enumerate(chunks):
        lanes = species * ck.slot
        outs = [struct((half, height, lanes), F32), struct((half, height, lanes), BF16)]
        own, sent = call(
            functools.partial(lat_kernel, ck, bands, height), outs, 1,
            scaled, lat_k, lat_s, perts[i], stds[i], *fields[i],
            scratch=[pltpu.VMEM((padded_total, lanes), F32)],
            flops=2 * 2 * 320 * 320 * lanes,
        )
        got = send(sent, "mem", 1)
        outs = [struct((height, lanes), F32)] + [struct((height, lanes), BF16)] * (half - 1)
        parts = call(pair_kernel, outs, 0, own, got)
        sums.append([parts[0]] + [send(parts[j], "mem", 2 * j) for j in range(1, half)])

    backs = []
    for i, ck in enumerate(chunks):
        lanes = species * ck.slot
        (g,) = call(
            functools.partial(pixel_kernel, ck, species), [struct((height, lanes), BF16)], 0,
            normals[i], *sums[i],
        )
        near = jnp.stack([g] + [send(g, "mem", 2 * j) for j in range(1, half)])
        far = send(near, "mem", 1)
        outs = [struct(((members + 1) * rows, lanes), BF16)] * bands
        got = call(
            functools.partial(back_kernel, ck, bands, half), outs, 1,
            scaled, lat_t, perts[i], stds[i], near, far,
            scratch=[pltpu.VMEM((padded_total, lanes), F32)],
            flops=2 * 3 * 320 * 320 * lanes,
        )
        backs += [got[0]] + [send(got[k], "band", k) for k in range(1, bands)]

    n = len(chunks)
    return tuple(
        pl.pallas_call(
            functools.partial(out_kernel, chunks, bands, species),
            grid=(species,),
            out_shape=[struct(alpha.shape, F32), struct(static_ctl.shape, F32)],
            in_specs=[
                pl.BlockSpec((members, 1, rows, lon), lambda s: (0, s, 0, 0)),
                pl.BlockSpec((1, rows, lon), lambda s: (s, 0, 0)),
            ]
            + [VMEM] * (n + n * bands),
            out_specs=[
                pl.BlockSpec((members, 1, rows, lon), lambda s: (0, s, 0, 0)),
                pl.BlockSpec((1, rows, lon), lambda s: (s, 0, 0)),
            ],
            compiler_params=pltpu.CompilerParams(vmem_limit_bytes=24 << 20),
            cost_estimate=pl.CostEstimate(flops=2 * 960 * 720 * 768, bytes_accessed=10**7, transcendentals=0),
        )(alpha, static_ctl, *roots, *backs)
    )


def solution(mesh):
    in_specs = (
        P("mem", None, "band", None),
        P(None, "band", None),
        P("mem", None, None, "band"),
        P(None, None, "band"),
        P(),
        P(),
        P(None, None, "mem", "band"),
        P("mem", "band"),
        P(None, "mem", "band"),
        P(),
        P(),
    )
    out_specs = (P("mem", None, "band", None), P(None, "band", None))
    body = functools.partial(shards, mesh.shape["band"], mesh.shape["mem"])
    return jax.shard_map(body, mesh=mesh, in_specs=in_specs, out_specs=out_specs, check_vma=False)
```

```python
import functools
import math

import jax
import jax.numpy as jnp
from jax import lax
from jax.experimental import pallas as pl
from jax.experimental.pallas import tpu as pltpu
from jax.sharding import PartitionSpec as P


F32 = jnp.float32
BF16 = jnp.bfloat16
VMEM = pl.BlockSpec(memory_space=pltpu.VMEM)
SMEM = pl.BlockSpec(memory_space=pltpu.SMEM)
NT = (((1,), (1,)), ((), ()))


def up(n, m):
    return -(-n // m) * m


def struct(shape, dtype):
    return jax.ShapeDtypeStruct(tuple(shape), dtype)


def call(kernel, outs, *args, smem=0, scratch=(), flops=10**8, vmem=24 << 20, spaces=None):
    size = sum(math.prod(a.shape) * a.dtype.itemsize for a in (*args, *outs))
    return pl.pallas_call(
        kernel,
        out_shape=outs,
        in_specs=[SMEM] * smem + [VMEM] * (len(args) - smem)
        if spaces is None
        else [pl.BlockSpec(memory_space=space) for space in spaces],
        out_specs=[VMEM] * len(outs),
        scratch_shapes=list(scratch),
        compiler_params=pltpu.CompilerParams(vmem_limit_bytes=vmem),
        cost_estimate=pl.CostEstimate(flops=flops, bytes_accessed=size, transcendentals=0),
    )(*args)


def dot(a, b):
    return jnp.dot(a, b, preferred_element_type=F32)


def dot_nt(a, b):
    return lax.dot_general(a, b, NT, preferred_element_type=F32)


def iota(shape, axis):
    return lax.broadcasted_iota(jnp.int32, shape, axis)


def one_hot(mask):
    return mask.astype(F32).astype(BF16)


def pack(pieces, start, width, slot):
    out = []
    for p in pieces:
        out.append(p[:, start : start + width])
        if slot > width:
            out.append(jnp.zeros((p.shape[0], slot - width), p.dtype))
    return jnp.concatenate(out, 1)


class Plan:
    def __init__(self, bands, ranks, alpha, lat_root):
        self.bands, self.ranks = bands, ranks
        self.members, self.species, self.rows, self.lon = alpha.shape
        self.lat = lat_root.shape[0]
        self.width = self.lon // bands // 2
        self.slot = up(self.width, 32)
        self.lanes = self.species * self.slot
        self.pixel = self.lat // ranks
        self.blocks = ranks // 2
        self.height = up(2 * self.pixel, 16)
        self.padded = self.blocks * self.height
        groups = math.gcd(ranks, self.rows)
        self.count, self.copies = self.rows // groups, ranks // groups
        self.extra = up(self.count, 16)
        self.late = self.members // 2


def factors(plan, weights, rank):
    total = weights[0] * weights[0]
    for i in range(1, weights.shape[0]):
        total = total + weights[i] * weights[i]
    norm = jnp.sqrt(jnp.full((1, plan.lanes), total.astype(F32)))
    return [
        0.8 * (jnp.full((1, plan.lanes), weights[rank * plan.members + m].astype(F32)) / norm)
        for m in range(plan.members)
    ]


def lon_kernel(plan, alpha, static, root, *refs):
    n = 2 * plan.bands
    x_refs, (a_buf, s_buf, r_buf, packed, sems) = refs[:n], refs[n:]
    species, rows, extra, members = plan.species, plan.rows, plan.extra, plan.members
    copies = [
        pltpu.make_async_copy(src, dst, sems.at[i])
        for i, (src, dst) in enumerate(((root, r_buf), (alpha, a_buf), (static, s_buf)))
    ]
    for copy in copies:
        copy.start()
    rank, me = lax.axis_index("mem"), lax.axis_index("band")
    t = iota((extra, rows), 0)
    mine = iota((extra, rows), 1) == (rank // plan.copies) * plan.count + t
    select = one_hot(mine & (t < plan.count) & (rank % plan.copies == 0))
    for copy in copies:
        copy.wait()
    fields = []
    for s in range(species):
        short = dot(select, s_buf[s]).astype(BF16)
        left = jnp.concatenate([a_buf[m, s] for m in range(members)] + [short], 0)
        fields.append(dot(left, r_buf[...]))
    for half in range(2):
        for b in range(plan.bands):
            at = (2 * b + half) * plan.width
            packed[half, b] = pack(fields, at, plan.width, plan.slot).astype(BF16)
    for own in range(2):
        half = (rank & 1) ^ 1 ^ own
        for k in range(plan.bands):
            x_refs[own * plan.bands + k][...] = packed[half, me ^ k]


def root_kernel(plan, root, w_ref):
    rank, me = lax.axis_index("mem"), lax.axis_index("band")
    side = plan.bands * plan.slot
    shape = (plan.lon, 2 * side)
    lane = iota(shape, 1)
    half = (lane // side) ^ 1 ^ (rank & 1)
    u = lane % plan.slot
    source = (lane % side // plan.slot ^ me) * (2 * plan.width) + half * plan.width + u
    pick = one_hot((iota(shape, 0) == source) & (u < plan.width))
    w_ref[...] = dot(root[...], pick).astype(BF16)


def prep_kernel(plan, pert, std, lat, perts_p, perts_o, std_p, std_o, lat_k, lat_t, lat_s):
    members, species, rows, total = plan.members, plan.species, plan.rows, plan.lat
    rank, me = lax.axis_index("mem"), lax.axis_index("band")
    for side in range(2):
        @pl.when(rank & 1 == side)
        def _():
            for half, p_ref, s_ref in ((1 - side, perts_p, std_p), (side, perts_o, std_o)):
                at = (half * plan.width, plan.width, plan.slot)
                for m in range(members):
                    pieces = [pert[m, s].astype(F32) for s in range(species)]
                    p_ref[m] = pack(pieces, *at).astype(BF16)
                s_ref[...] = 0.6 * pack([std[s] for s in range(species)], *at)
    row = iota((total, total), 0)
    order = one_hot(iota((total, total), 1) == (row // rows ^ me) * rows + row % rows)
    lat_k[...] = dot_nt(lat[...], order).astype(BF16)
    lat_t[...] = dot_nt(order, lat[...]).astype(BF16)
    row = iota((plan.bands * plan.extra, total), 0)
    t = row % plan.extra
    source = (row // plan.extra ^ me) * rows + (rank // plan.copies) * plan.count + t
    mine = iota((plan.bands * plan.extra, total), 1) == source
    pick = one_hot(mine & (t < plan.count) & (rank % plan.copies == 0))
    lat_s[...] = dot_nt(lat[...], pick).astype(BF16)


def normal_kernel(plan, error, jac, count, mask, h_p, h_o):
    channels, species, rows, lon = jac.shape
    rank = lax.axis_index("mem")
    pairs = [(s, t) for s in range(species) for t in range(s, species)]
    for r in range(0, rows, 8):
        n = min(8, rows - r)
        seen = count[r : r + n].astype(F32)

        def step(c, totals):
            weight = mask[c, r : r + n].astype(F32) * (seen * (1.0 / (error[c] * error[c])))
            j = [jac[c, s, r : r + n].astype(F32) for s in range(species)]
            scaled = [weight * x for x in j]
            return tuple(total + scaled[s] * j[t] for total, (s, t) in zip(totals, pairs))

        zero = tuple(jnp.zeros((n, lon), F32) for _ in pairs)
        sums = dict(zip(pairs, lax.fori_loop(0, channels, step, zero, unroll=2)))
        side = jnp.broadcast_to(rank & 1, (n, plan.width)) == 0
        for i, pair in enumerate(pairs):
            low, high = sums[pair][:, : plan.width], sums[pair][:, plan.width :]
            h_p[i, r : r + n, :] = jnp.where(side, high, low)
            h_o[i, r : r + n, :] = jnp.where(side, low, high)


def lat_kernel(plan, weights, lat_k, lat_s, pert, std, *refs):
    x_refs, out = refs[: plan.bands], refs[plan.bands]
    rows = plan.rows
    factor = factors(plan, weights, lax.axis_index("mem"))
    z = jnp.concatenate([x[plan.members * rows :, :] for x in x_refs], 0)
    acc = std[...] * dot(lat_s[...], z)
    for m in range(plan.members):
        z = jnp.concatenate([x[m * rows : (m + 1) * rows, :] for x in x_refs], 0)
        acc += factor[m] * pert[m].astype(F32) * dot(lat_k[...], z)
    out[...] = acc.astype(out.dtype)


def pair_kernel(plan, own, got, first, *refs):
    others, total = refs[:-1], refs[-1]
    block = lax.axis_index("mem") // 2
    total[...] = own[...] + got[...].astype(F32)
    for k, out in enumerate((first, *others)):
        at = pl.multiple_of((block ^ k) * plan.height, 8)
        out[...] = total[pl.ds(at, plan.height), :].astype(out.dtype)


def pixel_kernel(plan, h_own, h_got, first, *refs):
    got, out = refs[:-1], refs[-1]
    inc = first[...]
    for ref in got:
        inc = inc + ref[...].astype(F32)
    n, species = plan.pixel, plan.species
    pieces = [inc[:, t * plan.slot :][:, : plan.width] for t in range(species)]
    pairs = [(s, t) for s in range(species) for t in range(s, species)]
    rank = lax.axis_index("mem")
    for side in range(2):
        @pl.when(rank & 1 == side)
        def _():
            blocks = []
            for i, h in enumerate((h_own, h_got) if side == 0 else (h_got, h_own)):
                part = [p[i * n : (i + 1) * n] for p in pieces]
                sums = []
                for s in range(species):
                    terms = [h[pairs.index((min(s, t), max(s, t)))] * part[t] for t in range(species)]
                    sums.append(functools.reduce(jnp.add, terms))
                blocks.append(pack(sums, 0, plan.width, plan.slot))
            if plan.height > 2 * n:
                blocks.append(jnp.zeros((plan.height - 2 * n, plan.lanes), F32))
            out[...] = jnp.concatenate(blocks, 0).astype(BF16)


def back_kernel(plan, flip, weights, lat_t, pert, std, *refs):
    got, outs, full = refs[: plan.blocks], refs[plan.blocks : -1], refs[-1]
    rank, rows = lax.axis_index("mem"), plan.rows
    for k, ref in enumerate(got):
        at = pl.multiple_of((rank // 2 ^ k) * plan.height, 8)
        full[pl.ds(at, plan.height), :] = ref[...].astype(F32)
    g = full[...]
    factor = factors(plan, weights, rank ^ flip)
    for m in range(plan.members + 1):
        scale = factor[m] * pert[m].astype(F32) if m < plan.members else std[...]
        y = dot(lat_t[...], (scale * g).astype(BF16)).astype(BF16)
        late, at = m < plan.late, m - plan.late if m >= plan.late else m
        for k in range(plan.bands):
            outs[late * plan.bands + k][at * rows : (at + 1) * rows, :] = y[k * rows : (k + 1) * rows]


def product(plan, xs, w, fixed):
    at = fixed * plan.slot
    pieces = [x[:, at : at + plan.slot].astype(F32) for x in xs]
    return dot_nt(jnp.concatenate(pieces, 1).astype(BF16), w[...])


def early_kernel(plan, alpha, static, w, *refs):
    xs, (grad_alpha, grad_static) = refs[:-2], refs[-2:]
    rows, n = plan.rows, plan.members - plan.late
    for fixed in range(plan.species):
        @pl.when(pl.program_id(0) == fixed)
        def _():
            y = product(plan, xs, w, fixed)
            for m in range(n):
                grad_alpha[m, 0] = alpha[m, 0].astype(F32) + y[m * rows : (m + 1) * rows]
            grad_static[0] = static[0].astype(F32) + y[n * rows :]


def late_kernel(plan, _, alpha, w, *refs):
    xs, grad_alpha = refs[:-1], refs[-1]
    rows = plan.rows
    for fixed in range(plan.species):
        @pl.when(pl.program_id(0) == fixed)
        def _():
            y = product(plan, xs, w, fixed)
            for m in range(plan.late):
                grad_alpha[m, 0] = alpha[m, 0].astype(F32) + y[m * rows : (m + 1) * rows]


def shards(bands, ranks, *args):
    alpha, static_ctl, perturbations, static_std, lon_root, lat_root = args[:6]
    jacobian, obs_count, channel_mask, channel_error, member_weight = args[6:]
    plan = Plan(bands, ranks, alpha, lat_root)
    lanes, members, species = plan.lanes, plan.members, plan.species

    def send(x, axis, k):
        n = bands if axis == "band" else ranks
        return lax.ppermute(x, axis, [(i, i ^ k) for i in range(n)])

    def pad_lat(x, axis):
        if plan.height == 2 * plan.pixel:
            return x
        shape = list(x.shape)
        x = x.reshape(shape[:axis] + [plan.blocks, 2 * plan.pixel] + shape[axis + 1 :])
        widths = [(0, 0)] * x.ndim
        widths[axis + 1] = (0, plan.height - 2 * plan.pixel)
        shape[axis] = plan.padded
        return jnp.pad(x, widths).reshape(shape)

    sent = struct((members * plan.rows + plan.extra, lanes), BF16)
    got = call(
        functools.partial(lon_kernel, plan), [sent] * (2 * bands),
        alpha, static_ctl, lon_root, flops=10**9, spaces=[pl.ANY] * 3,
        scratch=[
            pltpu.VMEM(alpha.shape, BF16),
            pltpu.VMEM(static_ctl.shape, BF16),
            pltpu.VMEM(lon_root.shape, BF16),
            pltpu.VMEM((2, bands) + sent.shape, BF16),
            pltpu.SemaphoreType.DMA((3,)),
        ],
    )
    fields = [list(got[:bands]), list(got[bands:])]
    for own in range(2):
        fields[own][1:] = [send(fields[own][k], "band", k) for k in range(1, bands)]

    block = struct((plan.height, lanes), BF16)
    pert_shape = struct((members, plan.padded, lanes), BF16)
    std_shape = struct((plan.padded, lanes), F32)
    outs = [
        pert_shape, pert_shape, std_shape, std_shape,
        struct((plan.padded, plan.lat), BF16),
        struct((plan.lat, plan.padded), BF16),
        struct((plan.padded, bands * plan.extra), BF16),
    ]
    perts_p, perts_o, std_p, std_o, lat_k, lat_t, lat_s = call(
        functools.partial(prep_kernel, plan), outs,
        pad_lat(perturbations, 2), pad_lat(static_std, 1), pad_lat(lat_root, 0),
    )
    h_shape = struct((species * (species + 1) // 2, plan.pixel, plan.width), F32)
    h_p, h_o = call(
        functools.partial(normal_kernel, plan), [h_shape, h_shape],
        channel_error, jacobian, obs_count, channel_mask, smem=1,
    )
    h_got = send(h_p, "mem", 1)
    perts_got = send(perts_p, "mem", 1)

    sums = []
    for own, pert, std, kind in ((0, perts_p, std_p, BF16), (1, perts_o, std_o, F32)):
        sums += call(
            functools.partial(lat_kernel, plan), [struct((plan.padded, lanes), kind)],
            member_weight, lat_k, lat_s, pert, std, *fields[own], smem=1,
        )
    got = send(sums[0], "mem", 1)
    scratch = [pltpu.VMEM((plan.padded, lanes), F32)]
    parts = call(
        functools.partial(pair_kernel, plan),
        [struct((plan.height, lanes), F32)] + [block] * (plan.blocks - 1),
        sums[1], got, scratch=scratch,
    )
    parts = [parts[0]] + [send(parts[k], "mem", 2 * k) for k in range(1, plan.blocks)]
    (g,) = call(functools.partial(pixel_kernel, plan), [block], h_o, h_got, *parts)
    gs = [g] + [send(g, "mem", 2 * k) for k in range(1, plan.blocks)]

    (w,) = call(
        functools.partial(root_kernel, plan),
        [struct((plan.lon, 2 * bands * plan.slot), BF16)], lon_root, flops=10**9,
    )
    n_late = plan.late
    shapes = [struct(((members + 1 - n_late) * plan.rows, lanes), BF16)] * bands
    shapes += [struct((n_late * plan.rows, lanes), BF16)] * bands
    backs = {}
    for flip, pert in ((1, perts_got), (0, perts_o)):
        got = call(
            functools.partial(back_kernel, plan, flip), shapes,
            member_weight, lat_t, pert, std_o, *gs, smem=1, scratch=scratch,
        )
        for late in range(2):
            for k in range(bands):
                x = got[late * bands + k]
                if flip or k:
                    swap = [
                        (i * bands + j, (i ^ flip) * bands + (j ^ k))
                        for i in range(ranks)
                        for j in range(bands)
                    ]
                    x = lax.ppermute(x, ("mem", "band"), swap)
                backs[late, flip, k] = x
    early, last = [[backs[late, 1 - own, k] for own in range(2) for k in range(bands)] for late in range(2)]

    params = pltpu.CompilerParams(vmem_limit_bytes=24 << 20)
    cost = pl.CostEstimate(flops=10**9, bytes_accessed=10**7, transcendentals=0)
    n_early = members - n_late
    any_space = pl.BlockSpec(memory_space=pl.ANY)

    def block_of(n, first):
        return pl.BlockSpec((n, 1, plan.rows, plan.lon), lambda s: (first, s, 0, 0))

    static_block = pl.BlockSpec((1, plan.rows, plan.lon), lambda s: (s, 0, 0))
    grad_alpha, grad_static = pl.pallas_call(
        functools.partial(early_kernel, plan),
        grid=(species,),
        out_shape=[struct(alpha.shape, F32), struct(static_ctl.shape, F32)],
        in_specs=[block_of(n_early, 1), static_block] + [VMEM] * (1 + 2 * bands),
        out_specs=[block_of(n_early, 1), static_block],
        compiler_params=params, cost_estimate=cost, name="early",
    )(alpha, static_ctl, w, *early)
    grad_alpha = pl.pallas_call(
        functools.partial(late_kernel, plan),
        grid=(species,),
        out_shape=struct(alpha.shape, F32),
        in_specs=[any_space, block_of(n_late, 0)] + [VMEM] * (1 + 2 * bands),
        out_specs=block_of(n_late, 0),
        input_output_aliases={0: 0},
        compiler_params=params, cost_estimate=cost, name="late",
    )(grad_alpha, alpha, w, *last)
    return grad_alpha, grad_static


def solution(mesh):
    bands, ranks = mesh.shape["band"], mesh.shape["mem"]
    in_specs = (
        P("mem", None, "band", None),
        P(None, "band", None),
        P("mem", None, None, "band"),
        P(None, None, "band"),
        P(),
        P(),
        P(None, None, "mem", "band"),
        P("mem", "band"),
        P(None, "mem", "band"),
        P(),
        P(),
    )
    out_specs = (P("mem", None, "band", None), P(None, "band", None))

    def body(*args):
        return shards(bands, ranks, *args)

    return jax.shard_map(body, mesh=mesh, in_specs=in_specs, out_specs=out_specs, check_vma=False)
```

```python
import functools
import math

import jax
import jax.numpy as jnp
from jax import lax
from jax.experimental import pallas as pl
from jax.experimental.pallas import tpu as pltpu
from jax.sharding import PartitionSpec as P


F32 = jnp.float32
VMEM_BYTES = 67043328
BF16 = jnp.bfloat16
VMEM = pl.BlockSpec(memory_space=pltpu.VMEM)
SMEM = pl.BlockSpec(memory_space=pltpu.SMEM)
NT = (((1,), (1,)), ((), ()))


def up(n, m):
    return -(-n // m) * m


def struct(shape, dtype):
    return jax.ShapeDtypeStruct(tuple(shape), dtype)


def call(kernel, outs, *args, smem=0, scratch=(), flops=10**8, vmem=24 << 20, spaces=None):
    size = sum(math.prod(a.shape) * a.dtype.itemsize for a in (*args, *outs))
    return pl.pallas_call(
        kernel,
        out_shape=outs,
        in_specs=[SMEM] * smem + [VMEM] * (len(args) - smem)
        if spaces is None
        else [pl.BlockSpec(memory_space=space) for space in spaces],
        out_specs=[VMEM] * len(outs),
        scratch_shapes=list(scratch),
        compiler_params=pltpu.CompilerParams(vmem_limit_bytes=vmem),
        cost_estimate=pl.CostEstimate(flops=flops, bytes_accessed=size, transcendentals=0),
    )(*args)


def dot(a, b):
    return jnp.dot(a, b, preferred_element_type=F32)


def dot_nt(a, b):
    return lax.dot_general(a, b, NT, preferred_element_type=F32)


def iota(shape, axis):
    return lax.broadcasted_iota(jnp.int32, shape, axis)


def one_hot(mask):
    return mask.astype(F32).astype(BF16)


def pack(pieces, start, width, slot):
    out = []
    for p in pieces:
        out.append(p[:, start : start + width])
        if slot > width:
            out.append(jnp.zeros((p.shape[0], slot - width), p.dtype))
    return jnp.concatenate(out, 1)


class Plan:
    def __init__(self, bands, ranks, alpha, lat_root):
        self.bands, self.ranks = bands, ranks
        self.members, self.species, self.rows, self.lon = alpha.shape
        self.lat = lat_root.shape[0]
        self.width = self.lon // bands // 2
        self.slot = up(self.width, 32)
        self.lanes = self.species * self.slot
        self.pixel = self.lat // ranks
        self.blocks = ranks // 2
        self.height = up(2 * self.pixel, 16)
        self.padded = self.blocks * self.height
        groups = math.gcd(ranks, self.rows)
        self.count, self.copies = self.rows // groups, ranks // groups
        self.extra = up(self.count, 16)
        self.late = self.members // 2


def factors(plan, weights, rank):
    total = weights[0] * weights[0]
    for i in range(1, weights.shape[0]):
        total = total + weights[i] * weights[i]
    norm = jnp.sqrt(jnp.full((1, plan.lanes), total.astype(F32)))
    return [
        0.8 * (jnp.full((1, plan.lanes), weights[rank * plan.members + m].astype(F32)) / norm)
        for m in range(plan.members)
    ]


def lon_kernel(plan, alpha, static, root, lat, *refs):
    n = 2 * plan.bands
    x_refs, (lat_out, a_buf, s_buf, r_buf, packed, sems) = refs[:n], refs[n:]
    species, rows, extra, members = plan.species, plan.rows, plan.extra, plan.members
    moves = [(root, r_buf)] + [(alpha.at[m], a_buf.at[m]) for m in range(members)]
    moves += [(static, s_buf), (lat, lat_out)]
    copies = [pltpu.make_async_copy(src, dst, sems.at[i]) for i, (src, dst) in enumerate(moves)]
    for copy in copies:
        copy.start()
    rank, me = lax.axis_index("mem"), lax.axis_index("band")
    t = iota((extra, rows), 0)
    mine = iota((extra, rows), 1) == (rank // plan.copies) * plan.count + t
    select = one_hot(mine & (t < plan.count) & (rank % plan.copies == 0))
    for copy in copies:
        copy.wait()
    left = []
    for s in range(species):
        left += [a_buf[m, s] for m in range(members)] + [dot(select, s_buf[s]).astype(BF16)]
    y = dot(jnp.concatenate(left, 0), r_buf[...])
    size = members * rows + extra
    fields = [y[s * size : (s + 1) * size] for s in range(species)]
    for half in range(2):
        for b in range(plan.bands):
            at = (2 * b + half) * plan.width
            packed[half, b] = pack(fields, at, plan.width, plan.slot).astype(BF16)
    for own in range(2):
        half = (rank & 1) ^ 1 ^ own
        for k in range(plan.bands):
            x_refs[own * plan.bands + k][...] = packed[half, me ^ k]


def root_kernel(plan, root, lat, w_ref, lat_t):
    lat_t[...] = dot_nt(order_matrix(plan), lat[...]).astype(BF16)
    rank, me = lax.axis_index("mem"), lax.axis_index("band")
    side = plan.bands * plan.slot
    shape = (plan.lon, 2 * side)
    lane = iota(shape, 1)
    half = (lane // side) ^ 1 ^ (rank & 1)
    u = lane % plan.slot
    source = (lane % side // plan.slot ^ me) * (2 * plan.width) + half * plan.width + u
    pick = one_hot((iota(shape, 0) == source) & (u < plan.width))
    w_ref[...] = dot(root[...], pick).astype(BF16)


def prep_kernel(plan, own, pert, std, p_ref, s_ref):
    rank = lax.axis_index("mem")
    for side in range(2):
        @pl.when(rank & 1 == side)
        def _():
            half = side if own else 1 - side
            at = (half * plan.width, plan.width, plan.slot)
            for m in range(plan.members):
                pieces = [pert[m, s].astype(F32) for s in range(plan.species)]
                p_ref[m] = pack(pieces, *at).astype(BF16)
            s_ref[...] = 0.6 * pack([std[s] for s in range(plan.species)], *at)


def order_matrix(plan):
    row = iota((plan.lat, plan.lat), 0)
    source = (row // plan.rows ^ lax.axis_index("band")) * plan.rows + row % plan.rows
    return one_hot(iota((plan.lat, plan.lat), 1) == source)


def forward_kernel(plan, lat, lat_k, lat_s):
    rank, me = lax.axis_index("mem"), lax.axis_index("band")
    lat_k[...] = dot_nt(lat[...], order_matrix(plan)).astype(BF16)
    shape = (plan.bands * plan.extra, plan.lat)
    row = iota(shape, 0)
    t = row % plan.extra
    source = (row // plan.extra ^ me) * plan.rows + (rank // plan.copies) * plan.count + t
    pick = one_hot((iota(shape, 1) == source) & (t < plan.count) & (rank % plan.copies == 0))
    lat_s[...] = dot_nt(lat[...], pick).astype(BF16)


def normal_kernel(plan, error, jac, count, mask, h_p, h_o, inverse):
    channels, species, rows, lon = jac.shape
    rank = lax.axis_index("mem")
    pairs = [(s, t) for s in range(species) for t in range(s, species)]
    for c in range(channels):
        inverse[c] = 1.0 / (error[c] * error[c])
    for r in range(0, rows, 8):
        n = min(8, rows - r)
        seen = count[r : r + n].astype(F32)

        def step(c, totals):
            weight = mask[c, r : r + n].astype(F32) * (seen * inverse[c])
            j = [jac[c, s, r : r + n].astype(F32) for s in range(species)]
            scaled = [weight * x for x in j]
            return tuple(total + scaled[s] * j[t] for total, (s, t) in zip(totals, pairs))

        zero = tuple(jnp.zeros((n, lon), F32) for _ in pairs)
        sums = dict(zip(pairs, lax.fori_loop(0, channels, step, zero, unroll=8)))
        side = jnp.broadcast_to(rank & 1, (n, plan.width)) == 0
        for i, pair in enumerate(pairs):
            low, high = sums[pair][:, : plan.width], sums[pair][:, plan.width :]
            h_p[i, r : r + n, :] = jnp.where(side, high, low)
            h_o[i, r : r + n, :] = jnp.where(side, low, high)


def lat_kernel(plan, weights, lat_k, lat_s, pert, std, *refs):
    x_refs, out = refs[: plan.bands], refs[plan.bands]
    rows = plan.rows
    factor = factors(plan, weights, lax.axis_index("mem"))
    z = jnp.concatenate([x[plan.members * rows :, :] for x in x_refs], 0)
    acc = std[...] * dot(lat_s[...], z)
    for m in range(plan.members):
        z = jnp.concatenate([x[m * rows : (m + 1) * rows, :] for x in x_refs], 0)
        acc += factor[m] * pert[m].astype(F32) * dot(lat_k[...], z)
    out[...] = acc.astype(out.dtype)


def pair_kernel(plan, own, got, first, *refs):
    others, total = refs[:-1], refs[-1]
    block = lax.axis_index("mem") // 2
    total[...] = own[...] + got[...].astype(F32)
    for k, out in enumerate((first, *others)):
        at = pl.multiple_of((block ^ k) * plan.height, 8)
        out[...] = total[pl.ds(at, plan.height), :].astype(out.dtype)


def pixel_kernel(plan, h_own, h_got, first, *refs):
    got, out = refs[:-1], refs[-1]
    inc = first[...]
    for ref in got:
        inc = inc + ref[...].astype(F32)
    n, species = plan.pixel, plan.species
    pieces = [inc[:, t * plan.slot :][:, : plan.width] for t in range(species)]
    pairs = [(s, t) for s in range(species) for t in range(s, species)]
    rank = lax.axis_index("mem")
    for side in range(2):
        @pl.when(rank & 1 == side)
        def _():
            blocks = []
            for i, h in enumerate((h_own, h_got) if side == 0 else (h_got, h_own)):
                part = [p[i * n : (i + 1) * n] for p in pieces]
                sums = []
                for s in range(species):
                    terms = [h[pairs.index((min(s, t), max(s, t)))] * part[t] for t in range(species)]
                    sums.append(functools.reduce(jnp.add, terms))
                blocks.append(pack(sums, 0, plan.width, plan.slot))
            if plan.height > 2 * n:
                blocks.append(jnp.zeros((plan.height - 2 * n, plan.lanes), F32))
            out[...] = jnp.concatenate(blocks, 0).astype(BF16)


def back_kernel(plan, flip, weights, lat_t, pert, std, *refs):
    got, outs, full = refs[: plan.blocks], refs[plan.blocks : -1], refs[-1]
    rank, rows = lax.axis_index("mem"), plan.rows
    for k, ref in enumerate(got):
        at = pl.multiple_of((rank // 2 ^ k) * plan.height, 8)
        full[pl.ds(at, plan.height), :] = ref[...].astype(F32)
    g = full[...]
    factor = factors(plan, weights, rank ^ flip)
    for m in range(plan.members + 1):
        scale = factor[m] * pert[m].astype(F32) if m < plan.members else std[...]
        y = dot(lat_t[...], (scale * g).astype(BF16)).astype(BF16)
        late, at = m < plan.late, m - plan.late if m >= plan.late else m
        for k in range(plan.bands):
            outs[late * plan.bands + k][at * rows : (at + 1) * rows, :] = y[k * rows : (k + 1) * rows]


def product(plan, xs, w):
    rows = []
    for s in range(plan.species):
        pieces = [x[:, s * plan.slot : (s + 1) * plan.slot].astype(F32) for x in xs]
        rows.append(jnp.concatenate(pieces, 1).astype(BF16))
    return dot_nt(jnp.concatenate(rows, 0), w[...])


def finish(outs):
    copies = [pltpu.make_async_copy(src, dst, sem) for src, dst, sem in outs]
    for copy in copies:
        copy.start()
    return copies


def early_kernel(plan, alpha, static, w, *refs):
    xs, (grad_alpha, grad_static, a_buf, s_buf, sems) = refs[:-5], refs[-5:]
    rows, n, first = plan.rows, plan.members - plan.late, plan.late
    y = product(plan, xs, w)
    size, started = (n + 1) * rows, []
    for s in range(plan.species):
        for m in range(n):
            a_buf[m, s] = alpha[first + m, s].astype(F32) + y[s * size + m * rows :][:rows]
            started += finish([(a_buf.at[m, s], grad_alpha.at[first + m, s], sems.at[s, m])])
        s_buf[s] = static[s].astype(F32) + y[s * size + n * rows :][:rows]
        started += finish([(s_buf.at[s], grad_static.at[s], sems.at[s, n])])
    for copy in started:
        copy.wait()


def late_kernel(plan, _, alpha, w, *refs):
    xs, (grad_alpha, a_buf, sems) = refs[:-3], refs[-3:]
    rows, n = plan.rows, plan.late
    y = product(plan, xs, w)
    started = []
    for s in range(plan.species):
        for m in range(n):
            a_buf[m, s] = alpha[m, s].astype(F32) + y[(s * n + m) * rows :][:rows]
            started += finish([(a_buf.at[m, s], grad_alpha.at[m, s], sems.at[s, m])])
    for copy in started:
        copy.wait()


def shards(bands, ranks, *args):
    alpha, static_ctl, perturbations, static_std, lon_root, lat_root = args[:6]
    jacobian, obs_count, channel_mask, channel_error, member_weight = args[6:]
    plan = Plan(bands, ranks, alpha, lat_root)
    lanes, members, species = plan.lanes, plan.members, plan.species

    def send(x, axis, k):
        n = bands if axis == "band" else ranks
        return lax.ppermute(x, axis, [(i, i ^ k) for i in range(n)])

    def pad_lat(x, axis):
        if plan.height == 2 * plan.pixel:
            return x
        shape = list(x.shape)
        x = x.reshape(shape[:axis] + [plan.blocks, 2 * plan.pixel] + shape[axis + 1 :])
        widths = [(0, 0)] * x.ndim
        widths[axis + 1] = (0, plan.height - 2 * plan.pixel)
        shape[axis] = plan.padded
        return jnp.pad(x, widths).reshape(shape)

    sent = struct((members * plan.rows + plan.extra, lanes), BF16)
    lat = pad_lat(lat_root, 0)
    *got, lat = call(
        functools.partial(lon_kernel, plan), [sent] * (2 * bands) + [struct(lat.shape, BF16)],
        alpha, static_ctl, lon_root, lat, flops=10**9, spaces=[pltpu.HBM] * 4,
        vmem=VMEM_BYTES - 2 * (2 * bands * math.prod(sent.shape) + math.prod(lat.shape)) - (3 << 17),
        scratch=[
            pltpu.VMEM(alpha.shape, BF16),
            pltpu.VMEM(static_ctl.shape, BF16),
            pltpu.VMEM(lon_root.shape, BF16),
            pltpu.VMEM((2, bands) + sent.shape, BF16),
            pltpu.SemaphoreType.DMA((members + 3,)),
        ],
    )
    fields = [list(got[:bands]), list(got[bands:])]
    for own in range(2):
        fields[own][1:] = [send(fields[own][k], "band", k) for k in range(1, bands)]

    block = struct((plan.height, lanes), BF16)
    pert_shape = struct((members, plan.padded, lanes), BF16)
    std_shape = struct((plan.padded, lanes), F32)
    pert, std = pad_lat(perturbations, 2), pad_lat(static_std, 1)
    lat_k, lat_s = call(
        functools.partial(forward_kernel, plan),
        [struct((plan.padded, plan.lat), BF16), struct((plan.padded, bands * plan.extra), BF16)], lat,
    )
    perts_p, std_p = call(functools.partial(prep_kernel, plan, 0), [pert_shape, std_shape], pert, std)
    perts_o, std_o = call(functools.partial(prep_kernel, plan, 1), [pert_shape, std_shape], pert, std)
    h_shape = struct((species * (species + 1) // 2, plan.pixel, plan.width), F32)
    h_p, h_o = call(
        functools.partial(normal_kernel, plan), [h_shape, h_shape],
        channel_error, jacobian, obs_count, channel_mask, smem=1,
        scratch=[pltpu.SMEM(channel_error.shape, F32)],
    )
    h_got = send(h_p, "mem", 1)
    perts_got = send(perts_p, "mem", 1)

    sums = []
    for own, pert, std, kind in ((0, perts_p, std_p, BF16), (1, perts_o, std_o, F32)):
        sums += call(
            functools.partial(lat_kernel, plan), [struct((plan.padded, lanes), kind)],
            member_weight, lat_k, lat_s, pert, std, *fields[own], smem=1,
        )
    got = send(sums[0], "mem", 1)
    scratch = [pltpu.VMEM((plan.padded, lanes), F32)]
    parts = call(
        functools.partial(pair_kernel, plan),
        [struct((plan.height, lanes), F32)] + [block] * (plan.blocks - 1),
        sums[1], got, scratch=scratch,
    )
    parts = [parts[0]] + [send(parts[k], "mem", 2 * k) for k in range(1, plan.blocks)]
    (g,) = call(functools.partial(pixel_kernel, plan), [block], h_o, h_got, *parts)
    gs = [g] + [send(g, "mem", 2 * k) for k in range(1, plan.blocks)]

    w, lat_t = call(
        functools.partial(root_kernel, plan),
        [struct((plan.lon, 2 * bands * plan.slot), BF16), struct((plan.lat, plan.padded), BF16)],
        lon_root, lat, flops=10**9,
    )
    n_late = plan.late
    shapes = [struct(((members + 1 - n_late) * plan.rows, lanes), BF16)] * bands
    shapes += [struct((n_late * plan.rows, lanes), BF16)] * bands
    backs = {}
    for flip, pert in ((1, perts_got), (0, perts_o)):
        got = call(
            functools.partial(back_kernel, plan, flip), shapes,
            member_weight, lat_t, pert, std_o, *gs, smem=1, scratch=scratch,
        )
        for late in range(2):
            for k in range(bands):
                x = got[late * bands + k]
                if flip or k:
                    swap = [(i * bands + j, (i ^ flip) * bands + (j ^ k)) for i in range(ranks) for j in range(bands)]
                    x = lax.ppermute(x, ("mem", "band"), swap)
                backs[late, flip, k] = x
    early, last = [[backs[late, 1 - own, k] for own in range(2) for k in range(bands)] for late in range(2)]

    params = pltpu.CompilerParams(vmem_limit_bytes=24 << 20)
    cost = pl.CostEstimate(flops=10**9, bytes_accessed=10**7, transcendentals=0)
    n_early = members - n_late
    hbm = pl.BlockSpec(memory_space=pltpu.HBM)
    tile = (species, plan.rows, plan.lon)
    grad_alpha, grad_static = pl.pallas_call(
        functools.partial(early_kernel, plan),
        out_shape=[struct(alpha.shape, F32), struct(static_ctl.shape, F32)],
        in_specs=[VMEM] * (3 + 2 * bands),
        out_specs=[hbm, hbm],
        scratch_shapes=[
            pltpu.VMEM((n_early,) + tile, F32),
            pltpu.VMEM(tile, F32),
            pltpu.SemaphoreType.DMA((species, n_early + 1)),
        ],
        compiler_params=params, cost_estimate=cost, name="early",
    )(alpha, static_ctl, w, *early)
    grad_alpha = pl.pallas_call(
        functools.partial(late_kernel, plan),
        out_shape=struct(alpha.shape, F32),
        in_specs=[hbm] + [VMEM] * (2 + 2 * bands),
        out_specs=hbm,
        scratch_shapes=[pltpu.VMEM((n_late,) + tile, F32), pltpu.SemaphoreType.DMA((species, n_late))],
        input_output_aliases={0: 0},
        compiler_params=params, cost_estimate=cost, name="late",
    )(grad_alpha, alpha, w, *last)
    return grad_alpha, grad_static


def solution(mesh):
    bands, ranks = mesh.shape["band"], mesh.shape["mem"]
    in_specs = (
        P("mem", None, "band", None),
        P(None, "band", None),
        P("mem", None, None, "band"),
        P(None, None, "band"),
        P(),
        P(),
        P(None, None, "mem", "band"),
        P("mem", "band"),
        P(None, "mem", "band"),
        P(),
        P(),
    )
    out_specs = (P("mem", None, "band", None), P(None, "band", None))

    def body(*args):
        return shards(bands, ranks, *args)

    return jax.shard_map(body, mesh=mesh, in_specs=in_specs, out_specs=out_specs, check_vma=False)
```

```python
import functools
import math

import jax
import jax.numpy as jnp
from jax import lax
from jax.experimental import pallas as pl
from jax.experimental.pallas import tpu as pltpu
from jax.sharding import PartitionSpec as P


F32 = jnp.float32
VMEM_BYTES = 67043328
BF16 = jnp.bfloat16
VMEM = pl.BlockSpec(memory_space=pltpu.VMEM)
SMEM = pl.BlockSpec(memory_space=pltpu.SMEM)
NT = (((1,), (1,)), ((), ()))


def up(n, m):
    return -(-n // m) * m


def struct(shape, dtype):
    return jax.ShapeDtypeStruct(tuple(shape), dtype)


def call(kernel, outs, *args, smem=0, scratch=(), flops=10**8, vmem=24 << 20, spaces=None):
    size = sum(math.prod(a.shape) * a.dtype.itemsize for a in (*args, *outs))
    return pl.pallas_call(
        kernel,
        out_shape=outs,
        in_specs=[SMEM] * smem + [VMEM] * (len(args) - smem)
        if spaces is None
        else [pl.BlockSpec(memory_space=space) for space in spaces],
        out_specs=[VMEM] * len(outs),
        scratch_shapes=list(scratch),
        compiler_params=pltpu.CompilerParams(vmem_limit_bytes=vmem),
        cost_estimate=pl.CostEstimate(flops=flops, bytes_accessed=size, transcendentals=0),
    )(*args)


def dot(a, b):
    return jnp.dot(a, b, preferred_element_type=F32)


def dot_nt(a, b):
    return lax.dot_general(a, b, NT, preferred_element_type=F32)


def iota(shape, axis):
    return lax.broadcasted_iota(jnp.int32, shape, axis)


def one_hot(mask):
    return mask.astype(F32).astype(BF16)


def pack(pieces, start, width, slot):
    out = []
    for p in pieces:
        out.append(p[:, start : start + width])
        if slot > width:
            out.append(jnp.zeros((p.shape[0], slot - width), p.dtype))
    return jnp.concatenate(out, 1)


class Plan:
    def __init__(self, bands, ranks, alpha, lat_root):
        self.bands, self.ranks = bands, ranks
        self.members, self.species, self.rows, self.lon = alpha.shape
        self.lat = lat_root.shape[0]
        self.width = self.lon // bands // 2
        self.slot = up(self.width, 32)
        self.lanes = self.species * self.slot
        self.pixel = self.lat // ranks
        self.blocks = ranks // 2
        self.height = up(2 * self.pixel, 16)
        self.padded = self.blocks * self.height
        groups = math.gcd(ranks, self.rows)
        self.count, self.copies = self.rows // groups, ranks // groups
        self.extra = up(self.count, 16)
        self.late = self.members // 2


def factors(plan, weights, rank):
    total = weights[0] * weights[0]
    for i in range(1, weights.shape[0]):
        total = total + weights[i] * weights[i]
    norm = jnp.sqrt(jnp.full((1, plan.lanes), total.astype(F32)))
    return [
        0.8 * (jnp.full((1, plan.lanes), weights[rank * plan.members + m].astype(F32)) / norm)
        for m in range(plan.members)
    ]


def order_matrix(plan):
    row = iota((plan.lat, plan.lat), 0)
    source = (row // plan.rows ^ lax.axis_index("band")) * plan.rows + row % plan.rows
    return one_hot(iota((plan.lat, plan.lat), 1) == source)


def lon_kernel(plan, alpha, static, root, lat, *refs):
    n = 2 * plan.bands
    x_refs, (lat_k, lat_s, l_buf, a_buf, s_buf, r_buf, packed, sems) = refs[:n], refs[n:]
    species, rows, extra, members = plan.species, plan.rows, plan.extra, plan.members
    moves = [(lat, l_buf), (root, r_buf)] + [(alpha.at[m], a_buf.at[m]) for m in range(members)]
    moves.append((static, s_buf))
    copies = [pltpu.make_async_copy(src, dst, sems.at[i]) for i, (src, dst) in enumerate(moves)]
    for copy in copies:
        copy.start()
    rank, me = lax.axis_index("mem"), lax.axis_index("band")
    first = (rank // plan.copies) * plan.count
    t = iota((extra, rows), 0)
    select = one_hot((iota((extra, rows), 1) == first + t) & (t < plan.count) & (rank % plan.copies == 0))
    copies[0].wait()
    order = order_matrix(plan)
    lat_k[...] = dot_nt(l_buf[...], order).astype(BF16)
    shape = (plan.bands * extra, plan.lat)
    row = iota(shape, 0)
    t = row % extra
    source = (row // extra ^ me) * rows + first + t
    pick = one_hot((iota(shape, 1) == source) & (t < plan.count) & (rank % plan.copies == 0))
    lat_s[...] = dot_nt(l_buf[...], pick).astype(BF16)
    ys = []
    for copy in copies[1:-1]:
        copy.wait()
    half = members // 2
    left = [a_buf[m, s] for s in range(species) for m in range(half)]
    ys.append(dot(jnp.concatenate(left, 0), r_buf[...]))
    copies[-1].wait()
    left = []
    for s in range(species):
        left += [a_buf[m, s] for m in range(half, members)] + [dot(select, s_buf[s]).astype(BF16)]
    ys.append(dot(jnp.concatenate(left, 0), r_buf[...]))
    tops = (half * rows, (members - half) * rows + extra)
    at_row = 0
    for y, size in zip(ys, tops):
        fields = [y[s * size : (s + 1) * size] for s in range(species)]
        for h in range(2):
            for b in range(plan.bands):
                at = (2 * b + h) * plan.width
                packed[h, b, at_row : at_row + size, :] = pack(fields, at, plan.width, plan.slot).astype(BF16)
        at_row += size
    for own in range(2):
        h = (rank & 1) ^ 1 ^ own
        for k in range(plan.bands):
            x_refs[own * plan.bands + k][...] = packed[h, me ^ k]


def root_kernel(plan, root, lat, w_ref, lat_t):
    lat_t[...] = dot_nt(order_matrix(plan), lat[...]).astype(BF16)
    rank, me = lax.axis_index("mem"), lax.axis_index("band")
    side = plan.bands * plan.slot
    shape = (plan.lon, 2 * side)
    lane = iota(shape, 1)
    half = (lane // side) ^ 1 ^ (rank & 1)
    u = lane % plan.slot
    source = (lane % side // plan.slot ^ me) * (2 * plan.width) + half * plan.width + u
    pick = one_hot((iota(shape, 0) == source) & (u < plan.width))
    w_ref[...] = dot(root[...], pick).astype(BF16)


def prep_kernel(plan, own, pert, std, p_ref, s_ref):
    rank = lax.axis_index("mem")
    for side in range(2):
        @pl.when(rank & 1 == side)
        def _():
            half = side if own else 1 - side
            at = (half * plan.width, plan.width, plan.slot)
            for m in range(plan.members):
                pieces = [pert[m, s].astype(F32) for s in range(plan.species)]
                p_ref[m] = pack(pieces, *at).astype(BF16)
            s_ref[...] = 0.6 * pack([std[s].astype(F32) for s in range(plan.species)], *at)


def normal_kernel(plan, error, jac, count, mask, h_p, h_o, inverse):
    channels, species, rows, lon = jac.shape
    rank = lax.axis_index("mem")
    pairs = [(s, t) for s in range(species) for t in range(s, species)]
    for c in range(channels):
        inverse[c] = 1.0 / (error[c] * error[c])
    for r in range(0, rows, 8):
        n = min(8, rows - r)
        seen = count[r : r + n].astype(F32)

        def step(c, totals):
            weight = mask[c, r : r + n].astype(F32) * (seen * inverse[c])
            j = [jac[c, s, r : r + n].astype(F32) for s in range(species)]
            scaled = [weight * x for x in j]
            return tuple(total + scaled[s] * j[t] for total, (s, t) in zip(totals, pairs))

        zero = tuple(jnp.zeros((n, lon), F32) for _ in pairs)
        sums = dict(zip(pairs, lax.fori_loop(0, channels, step, zero, unroll=8)))
        side = jnp.broadcast_to(rank & 1, (n, plan.width)) == 0
        for i, pair in enumerate(pairs):
            low, high = sums[pair][:, : plan.width], sums[pair][:, plan.width :]
            h_p[i, r : r + n, :] = jnp.where(side, high, low).astype(BF16)
            h_o[i, r : r + n, :] = jnp.where(side, low, high)


def lat_kernel(plan, weights, lat_k, lat_s, pert, std, *refs):
    x_refs, outs = refs[: plan.bands], refs[plan.bands :]
    rows = plan.rows
    factor = factors(plan, weights, lax.axis_index("mem"))
    z = jnp.concatenate([x[plan.members * rows :, :] for x in x_refs], 0)
    acc = std[...] * dot(lat_s[...], z)
    for m in range(plan.members):
        z = jnp.concatenate([x[m * rows : (m + 1) * rows, :] for x in x_refs], 0)
        acc += factor[m] * pert[m].astype(F32) * dot(lat_k[...], z)
    if len(outs) == 1:
        outs[0][...] = acc
        return
    far, near, total = outs
    total[...] = acc
    side = lax.axis_index("mem") // plan.blocks
    n = plan.padded // 2
    far[...] = total[pl.ds(pl.multiple_of((side ^ 1) * n, 16), n), :].astype(BF16)
    near[...] = total[pl.ds(pl.multiple_of(side * n, 16), n), :].astype(BF16)


def pair_kernel(plan, far, own, got, *refs):
    outs, total = refs[:-1], refs[-1]
    block = lax.axis_index("mem") // 2
    n, half = plan.padded // 2, plan.blocks // 2
    side = block // half ^ far
    total[...] = own[pl.ds(pl.multiple_of(side * n, 16), n), :] + got[...].astype(F32)
    for k, out in enumerate(outs):
        at = pl.multiple_of((block % half ^ k) * plan.height, 8)
        out[...] = total[pl.ds(at, plan.height), :].astype(out.dtype)


def pixel_kernel(plan, h_own, h_got, first, *refs):
    got, out = refs[:-1], refs[-1]
    inc = first[...]
    for ref in got:
        inc = inc + ref[...].astype(F32)
    n, species = plan.pixel, plan.species
    pieces = [inc[:, t * plan.slot :][:, : plan.width] for t in range(species)]
    pairs = [(s, t) for s in range(species) for t in range(s, species)]
    rank = lax.axis_index("mem")
    for side in range(2):
        @pl.when(rank & 1 == side)
        def _():
            blocks = []
            for i, h in enumerate((h_own, h_got) if side == 0 else (h_got, h_own)):
                part = [p[i * n : (i + 1) * n] for p in pieces]
                sums = []
                for s in range(species):
                    terms = [h[pairs.index((min(s, t), max(s, t)))].astype(F32) * part[t] for t in range(species)]
                    sums.append(functools.reduce(jnp.add, terms))
                blocks.append(pack(sums, 0, plan.width, plan.slot))
            if plan.height > 2 * n:
                blocks.append(jnp.zeros((plan.height - 2 * n, plan.lanes), F32))
            out[...] = jnp.concatenate(blocks, 0).astype(BF16)


def back_kernel(plan, flip, weights, lat_t, pert, std, *refs):
    got, outs, full = refs[: plan.blocks], refs[plan.blocks : -1], refs[-1]
    rank, rows = lax.axis_index("mem"), plan.rows
    for k, ref in enumerate(got):
        at = pl.multiple_of((rank // 2 ^ k) * plan.height, 8)
        full[pl.ds(at, plan.height), :] = ref[...].astype(F32)
    g = full[...]
    factor = factors(plan, weights, rank ^ flip)
    for m in range(plan.members + 1):
        scale = factor[m] * pert[m].astype(F32) if m < plan.members else std[...]
        y = dot(lat_t[...], (scale * g).astype(BF16)).astype(BF16)
        late, at = m < plan.late, m - plan.late if m >= plan.late else m
        for k in range(plan.bands):
            outs[late * plan.bands + k][at * rows : (at + 1) * rows, :] = y[k * rows : (k + 1) * rows]


def product(plan, xs, w):
    rows = []
    for s in range(plan.species):
        pieces = [x[:, s * plan.slot : (s + 1) * plan.slot].astype(F32) for x in xs]
        rows.append(jnp.concatenate(pieces, 1).astype(BF16))
    return dot_nt(jnp.concatenate(rows, 0), w[...])


def finish(outs):
    copies = [pltpu.make_async_copy(src, dst, sem) for src, dst, sem in outs]
    for copy in copies:
        copy.start()
    return copies


def early_kernel(plan, alpha, static, w, *refs):
    xs, (grad_alpha, grad_static, a_buf, s_buf, sems) = refs[:-5], refs[-5:]
    rows, n, first = plan.rows, plan.members - plan.late, plan.late
    y = product(plan, xs, w)
    size, started = (n + 1) * rows, []
    for s in range(plan.species):
        for m in range(n):
            a_buf[m, s] = alpha[first + m, s].astype(F32) + y[s * size + m * rows :][:rows]
            started += finish([(a_buf.at[m, s], grad_alpha.at[first + m, s], sems.at[s, m])])
        s_buf[s] = static[s].astype(F32) + y[s * size + n * rows :][:rows]
        started += finish([(s_buf.at[s], grad_static.at[s], sems.at[s, n])])
    for copy in started:
        copy.wait()


def late_kernel(plan, _, alpha, w, *refs):
    xs, (grad_alpha, a_buf, sems) = refs[:-3], refs[-3:]
    rows, n = plan.rows, plan.late
    y = product(plan, xs, w)
    started = []
    for s in range(plan.species):
        for m in range(n):
            a_buf[m, s] = alpha[m, s].astype(F32) + y[(s * n + m) * rows :][:rows]
            started += finish([(a_buf.at[m, s], grad_alpha.at[m, s], sems.at[s, m])])
    for copy in started:
        copy.wait()


def shards(bands, ranks, *args):
    alpha, static_ctl, perturbations, static_std, lon_root, lat_root = args[:6]
    jacobian, obs_count, channel_mask, channel_error, member_weight = args[6:]
    plan = Plan(bands, ranks, alpha, lat_root)
    lanes, members, species = plan.lanes, plan.members, plan.species

    def send(x, axis, k):
        n = bands if axis == "band" else ranks
        return lax.ppermute(x, axis, [(i, i ^ k) for i in range(n)])

    def pad_lat(x, axis):
        if plan.height == 2 * plan.pixel:
            return x
        shape = list(x.shape)
        x = x.reshape(shape[:axis] + [plan.blocks, 2 * plan.pixel] + shape[axis + 1 :])
        widths = [(0, 0)] * x.ndim
        widths[axis + 1] = (0, plan.height - 2 * plan.pixel)
        shape[axis] = plan.padded
        return jnp.pad(x, widths).reshape(shape)

    sent = struct((members * plan.rows + plan.extra, lanes), BF16)
    lat = pad_lat(lat_root, 0)
    lat_shapes = [struct((plan.padded, plan.lat), BF16), struct((plan.padded, bands * plan.extra), BF16)]
    sizes = [sent.shape] * (2 * bands) + [(plan.padded, up(plan.lat, 128)), (plan.padded, 128)]
    *got, lat_k, lat_s = call(
        functools.partial(lon_kernel, plan), [sent] * (2 * bands) + lat_shapes,
        alpha, static_ctl, lon_root, lat, flops=10**9, spaces=[pltpu.HBM] * 4,
        vmem=VMEM_BYTES - 2 * sum(math.prod(size) for size in sizes) - (3 << 17),
        scratch=[
            pltpu.VMEM(lat.shape, BF16),
            pltpu.VMEM(alpha.shape, BF16),
            pltpu.VMEM(static_ctl.shape, BF16),
            pltpu.VMEM(lon_root.shape, BF16),
            pltpu.VMEM((2, bands) + sent.shape, BF16),
            pltpu.SemaphoreType.DMA((members + 3,)),
        ],
    )
    fields = [list(got[:bands]), list(got[bands:])]
    for own in range(2):
        fields[own][1:] = [send(fields[own][k], "band", k) for k in range(1, bands)]

    block = struct((plan.height, lanes), BF16)
    pert_shape = struct((members, plan.padded, lanes), BF16)
    std_shape = struct((plan.padded, lanes), F32)
    pert, std = pad_lat(perturbations, 2), pad_lat(static_std, 1)
    perts_p, std_p = call(functools.partial(prep_kernel, plan, 0), [pert_shape, std_shape], pert, std)
    perts_o, std_o = call(functools.partial(prep_kernel, plan, 1), [pert_shape, std_shape], pert, std)
    h_shape = struct((species * (species + 1) // 2, plan.pixel, plan.width), F32)
    h_p, h_o = call(
        functools.partial(normal_kernel, plan), [struct(h_shape.shape, BF16), h_shape],
        channel_error, jacobian, obs_count, channel_mask, smem=1,
        scratch=[pltpu.SMEM(channel_error.shape, F32)],
    )
    h_got = send(h_p, "mem", 1)
    perts_got = send(perts_p, "mem", 1)

    n = plan.padded // 2
    whole, part = pltpu.VMEM((plan.padded, lanes), F32), pltpu.VMEM((n, lanes), F32)
    far, near = call(
        functools.partial(lat_kernel, plan), [struct((n, lanes), BF16)] * 2,
        member_weight, lat_k, lat_s, perts_p, std_p, *fields[0], smem=1, scratch=[whole],
    )
    (own,) = call(
        functools.partial(lat_kernel, plan), [struct((plan.padded, lanes), F32)],
        member_weight, lat_k, lat_s, perts_o, std_o, *fields[1], smem=1,
    )
    half = plan.blocks // 2
    last = call(
        functools.partial(pair_kernel, plan, 1), [block] * half,
        own, send(far, "mem", 1), scratch=[part],
    )
    parts = call(
        functools.partial(pair_kernel, plan, 0),
        [struct((plan.height, lanes), F32)] + [block] * (half - 1),
        own, send(near, "mem", 1), scratch=[part],
    )
    parts = list(parts) + list(last)
    parts = [parts[0]] + [send(parts[k], "mem", 2 * k) for k in range(1, plan.blocks)]
    (g,) = call(functools.partial(pixel_kernel, plan), [block], h_o, h_got, *parts)
    gs = [g] + [send(g, "mem", 2 * k) for k in range(1, plan.blocks)]

    w, lat_t = call(
        functools.partial(root_kernel, plan),
        [struct((plan.lon, 2 * bands * plan.slot), BF16), struct((plan.lat, plan.padded), BF16)],
        lon_root, lat, flops=10**9,
    )
    n_late = plan.late
    shapes = [struct(((members + 1 - n_late) * plan.rows, lanes), BF16)] * bands
    shapes += [struct((n_late * plan.rows, lanes), BF16)] * bands
    backs = {}
    for flip, pert in ((1, perts_got), (0, perts_o)):
        got = call(
            functools.partial(back_kernel, plan, flip), shapes,
            member_weight, lat_t, pert, std_o, *gs, smem=1, scratch=[whole],
        )
        for late in range(2):
            for k in range(bands):
                x = got[late * bands + k]
                if flip or k:
                    swap = [(i * bands + j, (i ^ flip) * bands + (j ^ k)) for i in range(ranks) for j in range(bands)]
                    x = lax.ppermute(x, ("mem", "band"), swap)
                backs[late, flip, k] = x
    early, last = [[backs[late, 1 - own, k] for own in range(2) for k in range(bands)] for late in range(2)]

    params = pltpu.CompilerParams(vmem_limit_bytes=24 << 20)
    cost = pl.CostEstimate(flops=10**9, bytes_accessed=10**7, transcendentals=0)
    n_early = members - n_late
    hbm = pl.BlockSpec(memory_space=pltpu.HBM)
    tile = (species, plan.rows, plan.lon)
    grad_alpha, grad_static = pl.pallas_call(
        functools.partial(early_kernel, plan),
        out_shape=[struct(alpha.shape, F32), struct(static_ctl.shape, F32)],
        in_specs=[VMEM] * (3 + 2 * bands),
        out_specs=[hbm, hbm],
        scratch_shapes=[
            pltpu.VMEM((n_early,) + tile, F32),
            pltpu.VMEM(tile, F32),
            pltpu.SemaphoreType.DMA((species, n_early + 1)),
        ],
        compiler_params=params, cost_estimate=cost, name="early",
    )(alpha, static_ctl, w, *early)
    grad_alpha = pl.pallas_call(
        functools.partial(late_kernel, plan),
        out_shape=struct(alpha.shape, F32),
        in_specs=[hbm] + [VMEM] * (2 + 2 * bands),
        out_specs=hbm,
        scratch_shapes=[pltpu.VMEM((n_late,) + tile, F32), pltpu.SemaphoreType.DMA((species, n_late))],
        input_output_aliases={0: 0},
        compiler_params=params, cost_estimate=cost, name="late",
    )(grad_alpha, alpha, w, *last)
    return grad_alpha, grad_static


def solution(mesh):
    bands, ranks = mesh.shape["band"], mesh.shape["mem"]
    in_specs = (
        P("mem", None, "band", None),
        P(None, "band", None),
        P("mem", None, None, "band"),
        P(None, None, "band"),
        P(),
        P(),
        P(None, None, "mem", "band"),
        P("mem", "band"),
        P(None, "mem", "band"),
        P(),
        P(),
    )
    out_specs = (P("mem", None, "band", None), P(None, "band", None))

    def body(*args):
        return shards(bands, ranks, *args)

    return jax.shard_map(body, mesh=mesh, in_specs=in_specs, out_specs=out_specs, check_vma=False)
```

```python
import functools
import math

import jax
import jax.numpy as jnp
from jax import lax
from jax.experimental import pallas as pl
from jax.experimental.pallas import tpu as pltpu
from jax.sharding import PartitionSpec as P


F32 = jnp.float32
BF16 = jnp.bfloat16
VMEM = pl.BlockSpec(memory_space=pltpu.VMEM)
SMEM = pl.BlockSpec(memory_space=pltpu.SMEM)
NT = (((1,), (1,)), ((), ()))


def up(n, m):
    return -(-n // m) * m


def struct(shape, dtype):
    return jax.ShapeDtypeStruct(tuple(shape), dtype)


def call(kernel, outs, *args, smem=0, scratch=(), flops=10**8, vmem=14 << 20, spaces=None):
    size = sum(math.prod(a.shape) * a.dtype.itemsize for a in (*args, *outs))
    return pl.pallas_call(
        kernel,
        out_shape=outs,
        in_specs=[SMEM] * smem + [VMEM] * (len(args) - smem)
        if spaces is None
        else [pl.BlockSpec(memory_space=space) for space in spaces],
        out_specs=[VMEM] * len(outs),
        scratch_shapes=list(scratch),
        compiler_params=pltpu.CompilerParams(vmem_limit_bytes=vmem),
        cost_estimate=pl.CostEstimate(flops=flops, bytes_accessed=size, transcendentals=0),
    )(*args)


def dot(a, b):
    return jnp.dot(a, b, preferred_element_type=F32)


def dot_nt(a, b):
    return lax.dot_general(a, b, NT, preferred_element_type=F32)


def iota(shape, axis):
    return lax.broadcasted_iota(jnp.int32, shape, axis)


def one_hot(mask):
    return mask.astype(F32).astype(BF16)


def pack(pieces, start, width, slot):
    out = []
    for p in pieces:
        out.append(p[:, start : start + width])
        if slot > width:
            out.append(jnp.zeros((p.shape[0], slot - width), p.dtype))
    return jnp.concatenate(out, 1)


class Plan:
    def __init__(self, bands, ranks, alpha, lat_root):
        self.bands, self.ranks = bands, ranks
        self.members, self.species, self.rows, self.lon = alpha.shape
        self.lat = lat_root.shape[0]
        self.width = self.lon // bands // 2
        self.slot = up(self.width, 32)
        self.lanes = self.species * self.slot
        self.pixel = self.lat // ranks
        self.blocks = ranks // 2
        self.height = up(2 * self.pixel, 16)
        self.padded = self.blocks * self.height
        groups = math.gcd(ranks, self.rows)
        self.count, self.copies = self.rows // groups, ranks // groups
        self.extra = up(self.count, 16)
        self.late = self.members // 2


def factors(plan, weights, rank):
    total = weights[0] * weights[0]
    for i in range(1, weights.shape[0]):
        total = total + weights[i] * weights[i]
    norm = jnp.sqrt(jnp.full((1, plan.lanes), total.astype(F32)))
    return [
        0.8 * (jnp.full((1, plan.lanes), weights[rank * plan.members + m].astype(F32)) / norm)
        for m in range(plan.members)
    ]


def order_matrix(plan):
    row = iota((plan.lat, plan.lat), 0)
    source = (row // plan.rows ^ lax.axis_index("band")) * plan.rows + row % plan.rows
    return one_hot(iota((plan.lat, plan.lat), 1) == source)


def lon_kernel(plan, alpha, static, root, lat, *refs):
    n = 2 * plan.bands
    x_refs, (lat_k, lat_s, l_buf, a_buf, s_buf, r_buf, packed, sems) = refs[:n], refs[n:]
    species, rows, extra, members = plan.species, plan.rows, plan.extra, plan.members
    moves = [(lat, l_buf), (root, r_buf)] + [(alpha.at[m], a_buf.at[m]) for m in range(members)]
    moves.append((static, s_buf))
    copies = [pltpu.make_async_copy(src, dst, sems.at[i]) for i, (src, dst) in enumerate(moves)]
    for copy in copies:
        copy.start()
    rank, me = lax.axis_index("mem"), lax.axis_index("band")
    first = (rank // plan.copies) * plan.count
    t = iota((extra, rows), 0)
    select = one_hot((iota((extra, rows), 1) == first + t) & (t < plan.count) & (rank % plan.copies == 0))
    copies[0].wait()
    order = order_matrix(plan)
    lat_k[...] = dot_nt(l_buf[...], order).astype(BF16)
    shape = (plan.bands * extra, plan.lat)
    row = iota(shape, 0)
    t = row % extra
    source = (row // extra ^ me) * rows + first + t
    pick = one_hot((iota(shape, 1) == source) & (t < plan.count) & (rank % plan.copies == 0))
    lat_s[...] = dot_nt(l_buf[...], pick).astype(BF16)
    ys = []
    half = members // 2
    for copy in copies[1 : 2 + half]:
        copy.wait()
    left = [a_buf[m, s] for s in range(species) for m in range(half)]
    ys.append(dot(jnp.concatenate(left, 0), r_buf[...]))
    for copy in copies[2 + half :]:
        copy.wait()
    left = []
    for s in range(species):
        left += [a_buf[m, s] for m in range(half, members)] + [dot(select, s_buf[s]).astype(BF16)]
    ys.append(dot(jnp.concatenate(left, 0), r_buf[...]))
    tops = (half * rows, (members - half) * rows + extra)
    at_row = 0
    for y, size in zip(ys, tops):
        fields = [y[s * size : (s + 1) * size] for s in range(species)]
        for h in range(2):
            for b in range(plan.bands):
                at = (2 * b + h) * plan.width
                packed[h, b, at_row : at_row + size, :] = pack(fields, at, plan.width, plan.slot).astype(BF16)
        at_row += size
    for own in range(2):
        h = (rank & 1) ^ 1 ^ own
        for k in range(plan.bands):
            x_refs[own * plan.bands + k][...] = packed[h, me ^ k]


def root_kernel(plan, root, lat, w_ref, lat_t):
    lat_t[...] = dot_nt(order_matrix(plan), lat[...]).astype(BF16)
    rank, me = lax.axis_index("mem"), lax.axis_index("band")
    side = plan.bands * plan.slot
    shape = (plan.lon, 2 * side)
    lane = iota(shape, 1)
    half = (lane // side) ^ 1 ^ (rank & 1)
    u = lane % plan.slot
    source = (lane % side // plan.slot ^ me) * (2 * plan.width) + half * plan.width + u
    pick = one_hot((iota(shape, 0) == source) & (u < plan.width))
    w_ref[...] = dot(root[...], pick).astype(BF16)


def prep_kernel(plan, own, pert, std, p_ref, s_ref):
    rank = lax.axis_index("mem")
    for side in range(2):
        @pl.when(rank & 1 == side)
        def _():
            half = side if own else 1 - side
            at = (half * plan.width, plan.width, plan.slot)
            for m in range(plan.members):
                pieces = [pert[m, s].astype(F32) for s in range(plan.species)]
                p_ref[m] = pack(pieces, *at).astype(BF16)
            s_ref[...] = 0.6 * pack([std[s].astype(F32) for s in range(plan.species)], *at)


def normal_kernel(plan, error, jac, count, mask, h_p, h_o, inverse):
    channels, species, rows, lon = jac.shape
    rank = lax.axis_index("mem")
    pairs = [(s, t) for s in range(species) for t in range(s, species)]
    for c in range(channels):
        inverse[c] = 1.0 / (error[c] * error[c])
    for r in range(0, rows, 8):
        n = min(8, rows - r)
        seen = count[r : r + n].astype(F32)

        def step(c, totals):
            weight = mask[c, r : r + n].astype(F32) * (seen * inverse[c])
            j = [jac[c, s, r : r + n].astype(F32) for s in range(species)]
            scaled = [weight * x for x in j]
            return tuple(total + scaled[s] * j[t] for total, (s, t) in zip(totals, pairs))

        zero = tuple(jnp.zeros((n, lon), F32) for _ in pairs)
        sums = dict(zip(pairs, lax.fori_loop(0, channels, step, zero, unroll=16)))
        side = jnp.broadcast_to(rank & 1, (n, plan.width)) == 0
        for i, pair in enumerate(pairs):
            low, high = sums[pair][:, : plan.width], sums[pair][:, plan.width :]
            h_p[i, r : r + n, :] = jnp.where(side, high, low).astype(BF16)
            h_o[i, r : r + n, :] = jnp.where(side, low, high)


def lat_kernel(plan, weights, lat_k, lat_s, pert, std, *refs):
    x_refs, outs = refs[: plan.bands], refs[plan.bands :]
    rows = plan.rows
    factor = factors(plan, weights, lax.axis_index("mem"))
    z = jnp.concatenate([x[plan.members * rows :, :] for x in x_refs], 0)
    acc = std[...] * dot(lat_s[...], z)
    for m in range(plan.members):
        z = jnp.concatenate([x[m * rows : (m + 1) * rows, :] for x in x_refs], 0)
        acc += factor[m] * pert[m].astype(F32) * dot(lat_k[...], z)
    if len(outs) == 1:
        outs[0][...] = acc
        return
    far, near, total = outs
    total[...] = acc
    side = lax.axis_index("mem") // plan.blocks
    n = plan.padded // 2
    far[...] = total[pl.ds(pl.multiple_of((side ^ 1) * n, 16), n), :].astype(BF16)
    near[...] = total[pl.ds(pl.multiple_of(side * n, 16), n), :].astype(BF16)


def pair_kernel(plan, far, own, got, *refs):
    outs, total = refs[:-1], refs[-1]
    block = lax.axis_index("mem") // 2
    n, half = plan.padded // 2, plan.blocks // 2
    side = block // half ^ far
    total[...] = own[pl.ds(pl.multiple_of(side * n, 16), n), :] + got[...].astype(F32)
    for k, out in enumerate(outs):
        at = pl.multiple_of((block % half ^ k) * plan.height, 8)
        out[...] = total[pl.ds(at, plan.height), :].astype(out.dtype)


def pixel_kernel(plan, h_own, h_got, first, *refs):
    got, out = refs[:-1], refs[-1]
    inc = first[...]
    for ref in got:
        inc = inc + ref[...].astype(F32)
    n, species = plan.pixel, plan.species
    pieces = [inc[:, t * plan.slot :][:, : plan.width] for t in range(species)]
    pairs = [(s, t) for s in range(species) for t in range(s, species)]
    rank = lax.axis_index("mem")
    for side in range(2):
        @pl.when(rank & 1 == side)
        def _():
            blocks = []
            for i, h in enumerate((h_own, h_got) if side == 0 else (h_got, h_own)):
                part = [p[i * n : (i + 1) * n] for p in pieces]
                sums = []
                for s in range(species):
                    terms = [h[pairs.index((min(s, t), max(s, t)))].astype(F32) * part[t] for t in range(species)]
                    sums.append(functools.reduce(jnp.add, terms))
                blocks.append(pack(sums, 0, plan.width, plan.slot))
            if plan.height > 2 * n:
                blocks.append(jnp.zeros((plan.height - 2 * n, plan.lanes), F32))
            out[...] = jnp.concatenate(blocks, 0).astype(BF16)


def back_kernel(plan, flip, weights, lat_t, pert, std, *refs):
    got, outs, full = refs[: plan.blocks], refs[plan.blocks : -1], refs[-1]
    rank, rows = lax.axis_index("mem"), plan.rows
    for k, ref in enumerate(got):
        at = pl.multiple_of((rank // 2 ^ k) * plan.height, 8)
        full[pl.ds(at, plan.height), :] = ref[...].astype(F32)
    g = full[...]
    factor = factors(plan, weights, rank ^ flip)
    for m in range(plan.members + 1):
        scale = factor[m] * pert[m].astype(F32) if m < plan.members else std[...]
        y = dot(lat_t[...], (scale * g).astype(BF16)).astype(BF16)
        late, at = m < plan.late, m - plan.late if m >= plan.late else m
        for k in range(plan.bands):
            outs[late * plan.bands + k][at * rows : (at + 1) * rows, :] = y[k * rows : (k + 1) * rows]


def product(plan, xs, w):
    rows = []
    for s in range(plan.species):
        pieces = [x[:, s * plan.slot : (s + 1) * plan.slot].astype(F32) for x in xs]
        rows.append(jnp.concatenate(pieces, 1).astype(BF16))
    return dot_nt(jnp.concatenate(rows, 0), w[...])


def finish(outs):
    copies = [pltpu.make_async_copy(src, dst, sem) for src, dst, sem in outs]
    for copy in copies:
        copy.start()
    return copies


def early_kernel(plan, alpha, static, w, *refs):
    xs, (grad_alpha, grad_static, a_buf, s_buf, sems) = refs[:-5], refs[-5:]
    rows, n, first = plan.rows, plan.members - plan.late, plan.late
    y = product(plan, xs, w)
    size, started = (n + 1) * rows, []
    for s in range(plan.species):
        for m in range(n):
            a_buf[m, s] = alpha[first + m, s].astype(F32) + y[s * size + m * rows :][:rows]
            started += finish([(a_buf.at[m, s], grad_alpha.at[first + m, s], sems.at[s, m])])
        s_buf[s] = static[s].astype(F32) + y[s * size + n * rows :][:rows]
        started += finish([(s_buf.at[s], grad_static.at[s], sems.at[s, n])])
    for copy in started:
        copy.wait()


def late_kernel(plan, _, alpha, w, *refs):
    xs, (grad_alpha, a_buf, sems) = refs[:-3], refs[-3:]
    rows, n = plan.rows, plan.late
    y = product(plan, xs, w)
    started = []
    for s in range(plan.species):
        for m in range(n):
            a_buf[m, s] = alpha[m, s].astype(F32) + y[(s * n + m) * rows :][:rows]
            started += finish([(a_buf.at[m, s], grad_alpha.at[m, s], sems.at[s, m])])
    for copy in started:
        copy.wait()


def shards(bands, ranks, *args):
    alpha, static_ctl, perturbations, static_std, lon_root, lat_root = args[:6]
    jacobian, obs_count, channel_mask, channel_error, member_weight = args[6:]
    plan = Plan(bands, ranks, alpha, lat_root)
    lanes, members, species = plan.lanes, plan.members, plan.species

    def send(x, axis, k):
        n = bands if axis == "band" else ranks
        return lax.ppermute(x, axis, [(i, i ^ k) for i in range(n)])

    def pad_lat(x, axis):
        if plan.height == 2 * plan.pixel:
            return x
        shape = list(x.shape)
        x = x.reshape(shape[:axis] + [plan.blocks, 2 * plan.pixel] + shape[axis + 1 :])
        widths = [(0, 0)] * x.ndim
        widths[axis + 1] = (0, plan.height - 2 * plan.pixel)
        shape[axis] = plan.padded
        return jnp.pad(x, widths).reshape(shape)

    sent = struct((members * plan.rows + plan.extra, lanes), BF16)
    lat = pad_lat(lat_root, 0)
    lat_shapes = [struct((plan.padded, plan.lat), BF16), struct((plan.padded, bands * plan.extra), BF16)]
    *got, lat_k, lat_s = call(
        functools.partial(lon_kernel, plan), [sent] * (2 * bands) + lat_shapes,
        alpha, static_ctl, lon_root, lat, flops=10**9, spaces=[pltpu.HBM] * 4,
        vmem=53 << 20,
        scratch=[
            pltpu.VMEM(lat.shape, BF16),
            pltpu.VMEM(alpha.shape, BF16),
            pltpu.VMEM(static_ctl.shape, BF16),
            pltpu.VMEM(lon_root.shape, BF16),
            pltpu.VMEM((2, bands) + sent.shape, BF16),
            pltpu.SemaphoreType.DMA((members + 3,)),
        ],
    )
    fields = [list(got[:bands]), list(got[bands:])]
    for own in range(2):
        fields[own][1:] = [send(fields[own][k], "band", k) for k in range(1, bands)]

    block = struct((plan.height, lanes), BF16)
    pert_shape = struct((members, plan.padded, lanes), BF16)
    std_shape = struct((plan.padded, lanes), F32)
    pert, std = pad_lat(perturbations, 2), pad_lat(static_std, 1)
    perts_p, std_p = call(functools.partial(prep_kernel, plan, 0), [pert_shape, std_shape], pert, std)
    perts_o, std_o = call(functools.partial(prep_kernel, plan, 1), [pert_shape, std_shape], pert, std)
    h_shape = struct((species * (species + 1) // 2, plan.pixel, plan.width), F32)
    h_p, h_o = call(
        functools.partial(normal_kernel, plan), [struct(h_shape.shape, BF16), h_shape],
        channel_error, jacobian, obs_count, channel_mask, smem=1,
        scratch=[pltpu.SMEM(channel_error.shape, F32)],
    )
    h_got = send(h_p, "mem", 1)
    perts_got = send(perts_p, "mem", 1)

    n = plan.padded // 2
    whole, part = pltpu.VMEM((plan.padded, lanes), F32), pltpu.VMEM((n, lanes), F32)
    far, near = call(
        functools.partial(lat_kernel, plan), [struct((n, lanes), BF16)] * 2,
        member_weight, lat_k, lat_s, perts_p, std_p, *fields[0], smem=1, scratch=[whole],
    )
    (own,) = call(
        functools.partial(lat_kernel, plan), [struct((plan.padded, lanes), F32)],
        member_weight, lat_k, lat_s, perts_o, std_o, *fields[1], smem=1,
    )
    half = plan.blocks // 2
    last = call(
        functools.partial(pair_kernel, plan, 1), [block] * half,
        own, send(far, "mem", 1), scratch=[part],
    )
    parts = call(
        functools.partial(pair_kernel, plan, 0),
        [struct((plan.height, lanes), F32)] + [block] * (half - 1),
        own, send(near, "mem", 1), scratch=[part],
    )
    parts = list(parts) + list(last)
    parts = [parts[0]] + [send(parts[k], "mem", 2 * k) for k in range(1, plan.blocks)]
    (g,) = call(functools.partial(pixel_kernel, plan), [block], h_o, h_got, *parts)
    gs = [g] + [send(g, "mem", 2 * k) for k in range(1, plan.blocks)]

    w, lat_t = call(
        functools.partial(root_kernel, plan),
        [struct((plan.lon, 2 * bands * plan.slot), BF16), struct((plan.lat, plan.padded), BF16)],
        lon_root, lat, flops=10**9,
    )
    n_late = plan.late
    shapes = [struct(((members + 1 - n_late) * plan.rows, lanes), BF16)] * bands
    shapes += [struct((n_late * plan.rows, lanes), BF16)] * bands
    backs = {}
    for flip, pert in ((1, perts_got), (0, perts_o)):
        got = call(
            functools.partial(back_kernel, plan, flip), shapes,
            member_weight, lat_t, pert, std_o, *gs, smem=1, scratch=[whole],
        )
        for late in range(2):
            for k in range(bands):
                x = got[late * bands + k]
                if flip or k:
                    swap = [(i * bands + j, (i ^ flip) * bands + (j ^ k)) for i in range(ranks) for j in range(bands)]
                    x = lax.ppermute(x, ("mem", "band"), swap)
                backs[late, flip, k] = x
    early, last = [[backs[late, 1 - own, k] for own in range(2) for k in range(bands)] for late in range(2)]

    params = pltpu.CompilerParams(vmem_limit_bytes=20 << 20)
    cost = pl.CostEstimate(flops=10**9, bytes_accessed=10**7, transcendentals=0)
    n_early = members - n_late
    hbm = pl.BlockSpec(memory_space=pltpu.HBM)
    tile = (species, plan.rows, plan.lon)
    grad_alpha, grad_static = pl.pallas_call(
        functools.partial(early_kernel, plan),
        out_shape=[struct(alpha.shape, F32), struct(static_ctl.shape, F32)],
        in_specs=[VMEM] * (3 + 2 * bands),
        out_specs=[hbm, hbm],
        scratch_shapes=[
            pltpu.VMEM((n_early,) + tile, F32),
            pltpu.VMEM(tile, F32),
            pltpu.SemaphoreType.DMA((species, n_early + 1)),
        ],
        compiler_params=params, cost_estimate=cost, name="early",
    )(alpha, static_ctl, w, *early)
    grad_alpha = pl.pallas_call(
        functools.partial(late_kernel, plan),
        out_shape=struct(alpha.shape, F32),
        in_specs=[hbm] + [VMEM] * (2 + 2 * bands),
        out_specs=hbm,
        scratch_shapes=[pltpu.VMEM((n_late,) + tile, F32), pltpu.SemaphoreType.DMA((species, n_late))],
        input_output_aliases={0: 0},
        compiler_params=params, cost_estimate=cost, name="late",
    )(grad_alpha, alpha, w, *last)
    return grad_alpha, grad_static


def solution(mesh):
    bands, ranks = mesh.shape["band"], mesh.shape["mem"]
    in_specs = (
        P("mem", None, "band", None),
        P(None, "band", None),
        P("mem", None, None, "band"),
        P(None, None, "band"),
        P(),
        P(),
        P(None, None, "mem", "band"),
        P("mem", "band"),
        P(None, "mem", "band"),
        P(),
        P(),
    )
    out_specs = (P("mem", None, "band", None), P(None, "band", None))

    def body(*args):
        return shards(bands, ranks, *args)

    return jax.shard_map(body, mesh=mesh, in_specs=in_specs, out_specs=out_specs, check_vma=False)
```
